256 devices in a mesh: ctx: 32 (over z, x), head: 8 (over y, core).
Axes of the slice: x: 4, y: 4, z: 8, core: 2. Of those that a mesh axis runs over, the one named last changes fastest.
Arguments:
- projected: bfloat16 [3, 32768, 4096], P(None, ('ctx', 'head')), may hold values from -2.5 to 2.5
- conv_filter: float32 [3, 4, 4096], replicated, may hold values from -2.7 to 2.7
- frequencies: bfloat16 [32, 128, 256], replicated, may hold values from -5 to 5
Outputs:
- attended: bfloat16 [32768, 4096], P(('ctx', 'head'))
The draws below stay inside these ranges and needn't reach their ends.
All inputs are finite; a program needn't handle non-finite values.
Results may differ from the reference program's by a relative error of at most 0.013.
Values may be sent and summed in bfloat16 or wider, within the bound.
No kernel may reach another device: no remote copies, remote signals or barrier semaphores. Data moves between devices by JAX's collectives and lax.ppermute only.
A program may use at most 384 MiB of HBM per device.

```python
import jax
import jax.numpy as jnp
from jax import lax

H = 32
DH = 128
M = 256
KC = 4
BLOCK = 512
D = 4096
TOKENS = 32768


def shard_levels(stream_key, shape, cuts, least, top_value):
    loudness, own = 1.0, jax.random.fold_in(stream_key, 6)
    for axis_at, shards_of in cuts:
        heights = jnp.exp(jax.random.uniform(jax.random.fold_in(own, axis_at), (shards_of,), jnp.float32, least / len(cuts), top_value / len(cuts)))
        loudness = loudness * jnp.repeat(heights, shape[axis_at] // shards_of).reshape([-1 if axis == axis_at else 1 for axis in range(len(shape))])
    return loudness


def bell_draw(key, extent, spread, reach, cuts=(), held_as=jnp.bfloat16):
    level = shard_levels(key, extent, cuts, -0.22, 0.18) if cuts else 1.0
    result = jax.random.normal(key, extent, jnp.float32) * spread * level
    return jnp.minimum(jnp.maximum(result, -reach), reach).astype(held_as)


def setup_inputs(seed: int = 0) -> dict:
    key_list = jax.random.split(jax.random.key(seed), 4)
    return {
        "projected": bell_draw(key_list[0], (3, TOKENS, D), 1.0, 2.5, ((1, 256),)),
        "conv_filter": bell_draw(key_list[1], (3, KC, D), 0.45, 2.7, (), jnp.float32),
        "frequencies": bell_draw(key_list[2], (H, DH, M), 1.0, 5.0),
    }


def reference(projected, conv_filter, frequencies):
    block_count = TOKENS // BLOCK
    causal = jnp.arange(BLOCK)[:, None] >= jnp.arange(BLOCK)[None, :]
    feature_scale = DH ** -0.25

    def advance(carried, pieces):
        running_state_sum, key_total = carried
        block_of_queries, block_of_keys, value_block = pieces
        scores = jnp.dot(block_of_queries, block_of_keys.T, preferred_element_type=jnp.float32)
        scores = jnp.where(causal, scores, 0.0).astype(jnp.bfloat16)
        query_wide = block_of_queries.astype(jnp.float32)
        numerator = jnp.dot(scores, value_block, preferred_element_type=jnp.float32)
        numerator = numerator + jnp.dot(query_wide, running_state_sum, precision=lax.Precision.HIGHEST)
        denominator = jnp.sum(scores.astype(jnp.float32), axis=1) + jnp.dot(query_wide, key_total, precision=lax.Precision.HIGHEST)
        attended_output = (numerator / denominator[:, None]).astype(jnp.bfloat16)
        running_state_sum = running_state_sum + jnp.dot(block_of_keys.T, value_block, preferred_element_type=jnp.float32)
        key_total = key_total + jnp.sum(block_of_keys.astype(jnp.float32), axis=0)
        return (running_state_sum, key_total), attended_output

    def one_head(head_index):
        col_start = head_index * DH
        columns = lax.dynamic_slice_in_dim(projected, col_start, DH, 2).astype(jnp.float32)
        conv_taps = lax.dynamic_slice_in_dim(conv_filter, col_start, DH, 2)
        padded = jnp.pad(columns, ((0, 0), (KC - 1, 0), (0, 0)))
        summed = jnp.zeros_like(columns)
        for offset in range(KC):
            summed = summed + conv_taps[:, offset][:, None, :] * padded[:, KC - 1 - offset:KC - 1 - offset + TOKENS, :]
        conved = summed.astype(jnp.bfloat16)
        head_omega = frequencies[head_index]
        query_map = jnp.exp(jnp.dot(conved[0], head_omega, preferred_element_type=jnp.float32) * feature_scale).astype(jnp.bfloat16)
        keys_wide = conved[1].astype(jnp.float32)
        halfnorm = jnp.sum(keys_wide * keys_wide, axis=1, keepdims=True) * (0.5 * feature_scale * feature_scale)
        key_map = jnp.exp(jnp.dot(conved[1], head_omega, preferred_element_type=jnp.float32) * feature_scale - halfnorm).astype(jnp.bfloat16)
        initial = (jnp.zeros((M, DH), jnp.float32), jnp.zeros((M,), jnp.float32))
        pieces = (query_map.reshape(block_count, BLOCK, M), key_map.reshape(block_count, BLOCK, M), conved[2].reshape(block_count, BLOCK, DH))
        finals, output_list = lax.scan(advance, initial, pieces)
        return output_list.reshape(TOKENS, DH)

    per_head = lax.map(one_head, jnp.arange(H, dtype=jnp.int32))
    return jnp.transpose(per_head, (1, 0, 2)).reshape(TOKENS, H * DH)
```

```python
import functools

import jax
import jax.numpy as jnp
from jax import lax
from jax.experimental import pallas as pl
from jax.experimental.pallas import tpu as pltpu
from jax.sharding import Mesh
from jax.sharding import PartitionSpec as P

H = 32
DH = 128
M = 256
KC = 4
D = H * DH

CORES = 2
HEADS = H // CORES
COLS = HEADS * DH
ROWS = 128
CHUNK = CORES * ROWS
RIM = 8
PIECES = 2 * HEADS
STATE_ROWS = DH + 8
GROUP = 4
WIDE = GROUP * DH
STEPS = HEADS // GROUP
FEATURE_SCALE = DH ** (-0.25)
NORM_SCALE = 0.5 * FEATURE_SCALE * FEATURE_SCALE

AXES = ("zh", "zl", "x", "y", "c")
SIZES = (4, 2, 4, 4, 2)
PLANE = ("zl", "x", "y")

f32 = jnp.float32
bf16 = jnp.bfloat16
NT = (((1,), (1,)), ((), ()))


def dot(a, b):
    return jnp.dot(a, b, preferred_element_type=f32)


def dot_nt(a, b):
    return lax.dot_general(a, b, NT, preferred_element_type=f32)


def fill(core, own, other, rim_a, rim_b, rows):
    rows[0:RIM, :] = rim_a[0].astype(f32) + rim_b[0].astype(f32)
    rows[pl.ds(pl.multiple_of(RIM + core * ROWS, 8), ROWS), :] = own[0].astype(f32)
    rows[pl.ds(pl.multiple_of(RIM + (1 - core) * ROWS, 8), ROWS), :] = other[0].astype(f32)


def convolve(rows, taps, head):
    cols = slice(head * DH, (head + 1) * DH)
    summed = taps[0, 0:1, cols] * rows[RIM : RIM + CHUNK, cols]
    for j in range(1, KC):
        summed = summed + taps[0, j : j + 1, cols] * rows[RIM - j : RIM - j + CHUNK, cols]
    return summed.astype(bf16)


def keys_kernel(
    core_ref, own_k, own_v, other_k, other_v, rim_ka, rim_kb, rim_va, rim_vb, taps_k, taps_v,
    omega, state, key_map, values, rows_k, rows_v,
):
    core = core_ref[0]
    fill(core, own_k, other_k, rim_ka, rim_kb, rows_k)
    fill(core, own_v, other_v, rim_va, rim_vb, rows_v)
    ones = jnp.ones((M, M), bf16)
    for head in range(GROUP):
        k = convolve(rows_k, taps_k, head)
        v = convolve(rows_v, taps_v, head)
        k_wide = k.astype(f32)
        square = k_wide * k_wide
        upper = square.astype(bf16)
        lower = (square - upper.astype(f32)).astype(bf16)
        norm = dot(jnp.concatenate([upper, lower], axis=1), ones)
        mapped = jnp.exp(dot(k, omega[head]) * FEATURE_SCALE - norm * NORM_SCALE).astype(bf16)
        key_map[head] = mapped
        values[head] = v
        extended = jnp.concatenate([v.T, jnp.ones((16, CHUNK), bf16)], axis=0)
        sums = dot(extended, mapped)[:STATE_ROWS].astype(bf16)
        state[2 * head] = sums[:, : M // 2]
        state[2 * head + 1] = sums[:, M // 2 :]


def scores_kernel(
    core_ref, own_q, other_q, rim_qa, rim_qb, taps_q, omega, key_map, query_map, scores, rows_q
):
    core = core_ref[0]
    fill(core, own_q, other_q, rim_qa, rim_qb, rows_q)
    causal = lax.broadcasted_iota(jnp.int32, (CHUNK, CHUNK), 0) >= lax.broadcasted_iota(
        jnp.int32, (CHUNK, CHUNK), 1
    )
    for head in range(GROUP):
        q = convolve(rows_q, taps_q, head)
        mapped = jnp.exp(dot(q, omega[head]) * FEATURE_SCALE).astype(bf16)
        query_map[head] = mapped
        scores[head] = jnp.where(causal, dot_nt(mapped, key_map[head]), 0.0).astype(bf16)


def prefix_kernel(before_1, before_2, before_3, sums, out):
    running = before_1[...].astype(f32) + before_2[...].astype(f32) + before_3[...].astype(f32)
    for i in range(PIECES):
        out[i] = running.astype(bf16)
        running = running + sums[i].astype(f32)


def attend_kernel(core_ref, scores, query_map, values, state, out_own, out_other, rows):
    core = core_ref[0]
    ones = jnp.ones((CHUNK, DH), bf16)
    for head in range(GROUP):
        cols = slice(head * DH, (head + 1) * DH)
        prior = jnp.concatenate([state[2 * head], state[2 * head + 1]], axis=1)
        total = jnp.broadcast_to(prior[DH : DH + 1], (DH, M))
        prior = jnp.concatenate([prior[:DH], total], axis=0)
        both = dot(scores[head], jnp.concatenate([values[head], ones], axis=1))
        both = both + dot_nt(query_map[head], prior)
        rows[:, cols] = both[:, :DH] / both[:, DH:]
    out_own[...] = rows[pl.ds(pl.multiple_of(core * ROWS, 8), ROWS), :].astype(bf16)
    out_other[...] = rows[pl.ds(pl.multiple_of((1 - core) * ROWS, 8), ROWS), :].astype(bf16)


def spec(shape, index):
    return pl.BlockSpec(shape, index)


def own_spec(which):
    return spec((1, ROWS, WIDE), lambda i, core: (which, 0, core[0] * STEPS + i))


def other_spec(which):
    return spec((1, ROWS, WIDE), lambda i, core: (which, 0, i))


def rim_spec(which):
    return spec((1, RIM, WIDE), lambda i, core: (which, 0, i))


def taps_spec(which):
    return spec((1, KC, WIDE), lambda i, core: (which, 0, core[0] * STEPS + i))


OMEGA_SPEC = spec((GROUP, DH, M), lambda i, core: (core[0] * STEPS + i, 0, 0))


def head_spec(*dims):
    return spec((GROUP,) + dims, lambda i, core: (i,) + (0,) * len(dims))


STATE_SPEC = spec((2 * GROUP, STATE_ROWS, M // 2), lambda i, core: (i, 0, 0))
OUT_SPEC = spec((ROWS, WIDE), lambda i, core: (0, i))


def shape(*dims, dtype=bf16):
    return jax.ShapeDtypeStruct(dims, dtype)


def call(kernel, in_specs, out_specs, out_shape, scratch, flops, moved):
    return pl.pallas_call(
        kernel,
        grid_spec=pltpu.PrefetchScalarGridSpec(
            num_scalar_prefetch=1,
            grid=(STEPS,),
            in_specs=in_specs,
            out_specs=out_specs,
            scratch_shapes=scratch,
        ),
        out_shape=out_shape,
        compiler_params=pltpu.CompilerParams(
            dimension_semantics=("arbitrary",), vmem_limit_bytes=48 * 2**20
        ),
        cost_estimate=pl.CostEstimate(flops=flops, bytes_accessed=moved, transcendentals=0),
    )


def swap(array):
    return lax.ppermute(array, "c", [(0, 1), (1, 0)])


def per_device(projected, conv_filter, frequencies):
    core = lax.axis_index("c").astype(jnp.int32)
    cores = core.reshape(1)
    sent = lax.dynamic_slice_in_dim(projected, (1 - core) * COLS, COLS, 2)
    other = swap(sent)
    rim = projected[:, ROWS - RIM :, :]
    chips = ("zh", "zl", "x", "y", "c")
    count = 256 // CORES
    rims = [
        lax.ppermute(
            rim[:, :, to * COLS : (to + 1) * COLS],
            chips,
            [(2 * i + 1, 2 * (i + 1) + to) for i in range(count - 1)],
        )
        for to in range(CORES)
    ]
    state, key_map, values = call(
        keys_kernel,
        [own_spec(1), own_spec(2), other_spec(1), other_spec(2)]
        + [rim_spec(1), rim_spec(1), rim_spec(2), rim_spec(2)]
        + [taps_spec(1), taps_spec(2), OMEGA_SPEC],
        [STATE_SPEC, head_spec(CHUNK, M), head_spec(CHUNK, DH)],
        [shape(PIECES, STATE_ROWS, M // 2), shape(HEADS, CHUNK, M), shape(HEADS, CHUNK, DH)],
        [pltpu.VMEM((RIM + CHUNK, WIDE), f32)] * 2,
        flops=4 * 10**9,
        moved=10 * 2**20,
    )(
        cores, projected, projected, other, other, rims[0], rims[1], rims[0], rims[1],
        conv_filter, conv_filter, frequencies,
    )
    gathered = lax.all_to_all(state, PLANE, 0, 0, tiled=True)
    query_map, scores = call(
        scores_kernel,
        [own_spec(0), other_spec(0), rim_spec(0), rim_spec(0), taps_spec(0), OMEGA_SPEC]
        + [head_spec(CHUNK, M)],
        [head_spec(CHUNK, M), head_spec(CHUNK, CHUNK)],
        [shape(HEADS, CHUNK, M), shape(HEADS, CHUNK, CHUNK)],
        [pltpu.VMEM((RIM + CHUNK, WIDE), f32)],
        flops=8 * 10**9,
        moved=20 * 2**20,
    )(cores, projected, other, rims[0], rims[1], conv_filter, frequencies, key_map)
    total = jnp.sum(gathered.astype(f32), axis=0).astype(bf16)
    planes = SIZES[0]
    before = [
        lax.ppermute(total, "zh", [(i, i + by) for i in range(planes - by)])
        for by in range(1, planes)
    ]
    prior = pl.pallas_call(
        prefix_kernel,
        out_shape=shape(PIECES, STATE_ROWS, M // 2),
        compiler_params=pltpu.CompilerParams(vmem_limit_bytes=16 * 2**20),
    )(*before, gathered)
    prior = lax.all_to_all(prior, PLANE, 0, 0, tiled=True)
    out_own, out_other = call(
        attend_kernel,
        [head_spec(CHUNK, CHUNK), head_spec(CHUNK, M), head_spec(CHUNK, DH), STATE_SPEC],
        [OUT_SPEC, OUT_SPEC],
        [shape(ROWS, COLS), shape(ROWS, COLS)],
        [pltpu.VMEM((CHUNK, WIDE), f32)],
        flops=4 * 10**9,
        moved=8 * 2**20,
    )(cores, scores, query_map, values, prior)
    arrived = swap(out_other)
    first = jnp.where(core == 0, out_own, arrived)
    second = jnp.where(core == 0, arrived, out_own)
    return jnp.concatenate([first, second], axis=1)


def solution(mesh):
    devices = Mesh(mesh.devices.reshape(SIZES), AXES)
    placed = (P(None, AXES, None), P(), P())
    return jax.shard_map(
        per_device, mesh=devices, in_specs=placed, out_specs=P(AXES, None), check_vma=False
    )
```

```python
import functools

import jax
import jax.numpy as jnp
from jax import lax
from jax.experimental import pallas as pl
from jax.experimental.pallas import tpu as pltpu
from jax.sharding import Mesh
from jax.sharding import PartitionSpec as P

H = 32
DH = 128
M = 256
KC = 4
D = H * DH

CORES = 2
HEADS = H // CORES
COLS = HEADS * DH
ROWS = 128
CHUNK = CORES * ROWS
RIM = 8
PIECES = 2 * HEADS
STATE_ROWS = DH + 8
GROUP = 4
WIDE = GROUP * DH
STEPS = HEADS // GROUP
FEATURE_SCALE = DH ** (-0.25)
NORM_SCALE = 0.5 * FEATURE_SCALE * FEATURE_SCALE

AXES = ("zh", "zl", "x", "y", "c")
SIZES = (4, 2, 4, 4, 2)
PLANE = ("zl", "x", "y")

f32 = jnp.float32
bf16 = jnp.bfloat16
NT = (((1,), (1,)), ((), ()))


def dot(a, b):
    return jnp.dot(a, b, preferred_element_type=f32)


def dot_nt(a, b):
    return lax.dot_general(a, b, NT, preferred_element_type=f32)


def fill(core, own, other, rim_a, rim_b, rows):
    rows[0:RIM, :] = rim_a[0].astype(f32) + rim_b[0].astype(f32)
    rows[pl.ds(pl.multiple_of(RIM + core * ROWS, 8), ROWS), :] = own[0].astype(f32)
    rows[pl.ds(pl.multiple_of(RIM + (1 - core) * ROWS, 8), ROWS), :] = other[0].astype(f32)


def convolve(rows, taps, head):
    cols = slice(head * DH, (head + 1) * DH)
    summed = taps[0, 0:1, cols] * rows[RIM : RIM + CHUNK, cols]
    for j in range(1, KC):
        summed = summed + taps[0, j : j + 1, cols] * rows[RIM - j : RIM - j + CHUNK, cols]
    return summed.astype(bf16)


def keys_kernel(
    core_ref, own, other, rim_a, rim_b, taps, omega,
    state, key_map, values, rows_k, rows_v, maps, convolved, sems,
):
    core = core_ref[0]
    ones = jnp.ones((M, M), bf16)

    def copies(group):
        heads = pl.ds(group * GROUP, GROUP)
        return (
            pltpu.make_async_copy(maps.at[heads], key_map.at[heads], sems.at[0, group]),
            pltpu.make_async_copy(convolved.at[heads], values.at[heads], sems.at[1, group]),
        )

    def one(group, carried):
        cols = columns(group * WIDE, WIDE)
        for which, rows in ((0, rows_k), (1, rows_v)):
            fill(
                core,
                own.at[pl.ds(which, 1), :, cols],
                other.at[pl.ds(which, 1), :, cols],
                rim_a.at[pl.ds(which + 1, 1), :, cols],
                rim_b.at[pl.ds(which + 1, 1), :, cols],
                rows,
            )
        for part in range(GROUP):
            head = group * GROUP + part
            k = convolve(rows_k, taps.at[pl.ds(1, 1), :, cols], part)
            v = convolve(rows_v, taps.at[pl.ds(2, 1), :, cols], part)
            k_wide = k.astype(f32)
            square = k_wide * k_wide
            upper = square.astype(bf16)
            lower = (square - upper.astype(f32)).astype(bf16)
            norm = dot(jnp.concatenate([upper, lower], axis=1), ones)
            mapped = jnp.exp(dot(k, omega[head]) * FEATURE_SCALE - norm * NORM_SCALE).astype(bf16)
            maps[head] = mapped
            convolved[head] = v
            extended = jnp.concatenate([v.T, jnp.ones((16, CHUNK), bf16)], axis=0)
            sums = dot(extended, mapped)[:STATE_ROWS].astype(bf16)
            state[2 * head] = sums[:, : M // 2]
            state[2 * head + 1] = sums[:, M // 2 :]
        for copy in copies(group):
            copy.start()
        return carried

    lax.fori_loop(0, STEPS, one, 0)
    for group in range(STEPS):
        for copy in copies(group):
            copy.wait()


def scores_kernel(
    core_ref, own_q, other_q, rim_qa, rim_qb, taps_q, omega, key_map, query_map, scores, rows_q
):
    core = core_ref[0]
    fill(core, own_q, other_q, rim_qa, rim_qb, rows_q)
    causal = lax.broadcasted_iota(jnp.int32, (CHUNK, CHUNK), 0) >= lax.broadcasted_iota(
        jnp.int32, (CHUNK, CHUNK), 1
    )
    for head in range(GROUP):
        q = convolve(rows_q, taps_q, head)
        mapped = jnp.exp(dot(q, omega[head]) * FEATURE_SCALE).astype(bf16)
        query_map[head] = mapped
        scores[head] = jnp.where(causal, dot_nt(mapped, key_map[head]), 0.0).astype(bf16)


def total_kernel(sums, out):
    total = sums[0].astype(f32)
    for i in range(1, PIECES):
        total = total + sums[i].astype(f32)
    out[...] = total.astype(bf16)


def prefix_kernel(before_1, before_2, before_3, sums, out):
    running = before_1[...].astype(f32) + before_2[...].astype(f32) + before_3[...].astype(f32)
    for i in range(PIECES):
        out[i] = running.astype(bf16)
        running = running + sums[i].astype(f32)


def attend_rows(rows, scores, query_map, values, state, put):
    ones = jnp.ones((CHUNK, DH), bf16)

    def one(head, carried):
        prior = jnp.concatenate([state[2 * head], state[2 * head + 1]], axis=1)
        total = jnp.broadcast_to(prior[DH : DH + 1], (DH, M))
        prior = jnp.concatenate([prior[:DH], total], axis=0)
        both = dot(scores[head, rows, :], jnp.concatenate([values[head], ones], axis=1))
        both = both + dot_nt(query_map[head, rows, :], prior)
        put(head, (both[:, :DH] / both[:, DH:]).astype(bf16))
        return carried

    lax.fori_loop(0, HEADS, one, 0, unroll=4)


def columns(start, size):
    return pl.ds(pl.multiple_of(start, DH), size)


def attend_other_kernel(core_ref, scores, query_map, values, state, out):
    start = pl.multiple_of((1 - core_ref[0]) * ROWS, ROWS)

    def put(head, block):
        out[:, columns(head * DH, DH)] = block

    attend_rows(pl.ds(start, ROWS), scores, query_map, values, state, put)


def attend_own_kernel(core_ref, scores, query_map, values, state, out, block_rows, sem):
    core = core_ref[0]
    start = pl.multiple_of(core * ROWS, ROWS)

    def put(head, block):
        block_rows[:, columns(head * DH, DH)] = block

    attend_rows(pl.ds(start, ROWS), scores, query_map, values, state, put)
    copy = pltpu.make_async_copy(block_rows, out.at[:, columns(core * COLS, COLS)], sem)
    copy.start()
    copy.wait()


def finish_kernel(core_ref, arrived, partial, out, sem):
    copy = pltpu.make_async_copy(arrived, out.at[:, columns((1 - core_ref[0]) * COLS, COLS)], sem)
    copy.start()
    copy.wait()


def run_copies(pairs, sems):
    copies = [
        pltpu.make_async_copy(source, target, sems.at[i])
        for i, (source, target) in enumerate(pairs)
    ]
    for copy in copies:
        copy.start()
    for copy in copies:
        copy.wait()


def split_kernel(core_ref, projected, rim_a, rim_b, sent, sent_q, sems):
    cols = columns((1 - core_ref[0]) * COLS, COLS)
    last = pl.ds(ROWS - RIM, RIM)
    pairs = [
        (projected.at[:, last, pl.ds(0, COLS)], rim_a),
        (projected.at[:, last, pl.ds(COLS, COLS)], rim_b),
        (projected.at[pl.ds(1, 2), :, cols], sent),
        (projected.at[pl.ds(0, 1), :, cols], sent_q),
    ]
    run_copies(pairs, sems)


def fetch_kernel(core_ref, projected, taps, omega, own, own_taps, own_omega, sems):
    cols = columns(core_ref[0] * COLS, COLS)
    pairs = [
        (projected.at[pl.ds(1, 2), :, cols], own),
        (taps.at[:, :, cols], own_taps),
        (omega.at[pl.ds(core_ref[0] * HEADS, HEADS)], own_omega),
    ]
    run_copies(pairs, sems)


def spec(shape, index):
    return pl.BlockSpec(shape, index)


def own_spec(which):
    return spec((1, ROWS, WIDE), lambda i, core: (which, 0, core[0] * STEPS + i))


def other_spec(which):
    return spec((1, ROWS, WIDE), lambda i, core: (which, 0, i))


def rim_spec(which):
    return spec((1, RIM, WIDE), lambda i, core: (which, 0, i))


def taps_spec(which):
    return spec((1, KC, WIDE), lambda i, core: (which, 0, core[0] * STEPS + i))


OMEGA_SPEC = spec((GROUP, DH, M), lambda i, core: (core[0] * STEPS + i, 0, 0))


def head_spec(*dims):
    return spec((GROUP,) + dims, lambda i, core: (i,) + (0,) * len(dims))


STATE_SPEC = spec((2 * GROUP, STATE_ROWS, M // 2), lambda i, core: (i, 0, 0))
SCALAR = pl.BlockSpec(memory_space=pltpu.SMEM)
WHOLE = pl.BlockSpec(memory_space=pltpu.VMEM)
ANYWHERE = pl.BlockSpec(memory_space=pl.ANY)


def chip(*dims):
    return pltpu.VMEM(dims, bf16)


def main(*dims):
    return pltpu.HBM(dims, bf16)


def in_chip(*arrays):
    return [pltpu.with_memory_space_constraint(a, pltpu.VMEM) for a in arrays]


def in_main(*arrays):
    return [pltpu.with_memory_space_constraint(a, pltpu.HBM) for a in arrays]


def small_call(kernel, in_specs, out_specs, out_shape, scratch, flops, moved, aliases=None):
    return pl.pallas_call(
        kernel,
        in_specs=in_specs,
        out_specs=out_specs,
        out_shape=out_shape,
        scratch_shapes=scratch,
        input_output_aliases=aliases or {},
        compiler_params=pltpu.CompilerParams(vmem_limit_bytes=16 * 2**20),
        cost_estimate=pl.CostEstimate(flops=flops, bytes_accessed=moved, transcendentals=0),
    )


def call(kernel, in_specs, out_specs, out_shape, scratch, flops, moved):
    return pl.pallas_call(
        kernel,
        grid_spec=pltpu.PrefetchScalarGridSpec(
            num_scalar_prefetch=1,
            grid=(STEPS,),
            in_specs=in_specs,
            out_specs=out_specs,
            scratch_shapes=scratch,
        ),
        out_shape=out_shape,
        compiler_params=pltpu.CompilerParams(
            dimension_semantics=("arbitrary",), vmem_limit_bytes=20 * 2**20
        ),
        cost_estimate=pl.CostEstimate(flops=flops, bytes_accessed=moved, transcendentals=0),
    )


def swap(array):
    return lax.ppermute(array, "c", [(0, 1), (1, 0)])


def per_device(projected, conv_filter, frequencies):
    core = lax.axis_index("c").astype(jnp.int32)
    cores = core.reshape(1)
    projected, conv_filter, frequencies = in_main(projected, conv_filter, frequencies)
    *halves, sent, sent_q = small_call(
        split_kernel,
        [SCALAR, ANYWHERE],
        [WHOLE] * 4,
        [chip(3, RIM, COLS), chip(3, RIM, COLS), chip(2, ROWS, COLS), chip(1, ROWS, COLS)],
        [pltpu.SemaphoreType.DMA((4,))],
        flops=0,
        moved=3 * 2**20,
    )(cores, projected)
    count = 256 // CORES
    rims = [
        lax.ppermute(
            halves[to], AXES, [(2 * i + 1, 2 * (i + 1) + to) for i in range(count - 1)]
        )
        for to in range(CORES)
    ]
    other, other_q = swap(sent), swap(sent_q)
    fetched = small_call(
        fetch_kernel,
        [SCALAR] + [ANYWHERE] * 3,
        [WHOLE] * 3,
        [chip(2, ROWS, COLS), pltpu.VMEM((3, KC, COLS), f32), chip(HEADS, DH, M)],
        [pltpu.SemaphoreType.DMA((3,))],
        flops=0,
        moved=5 * 2**20,
    )(cores, projected, conv_filter, frequencies)
    own, own_taps, own_omega, other, *rims = in_chip(*fetched, other, *rims)
    state, key_map, values = small_call(
        keys_kernel,
        [SCALAR] + [WHOLE] * 6,
        [WHOLE, ANYWHERE, ANYWHERE],
        [chip(PIECES, STATE_ROWS, M // 2), main(HEADS, CHUNK, M), main(HEADS, CHUNK, DH)],
        [pltpu.VMEM((RIM + CHUNK, WIDE), f32)] * 2
        + [pltpu.VMEM((HEADS, CHUNK, M), bf16), pltpu.VMEM((HEADS, CHUNK, DH), bf16)]
        + [pltpu.SemaphoreType.DMA((2, STEPS))],
        flops=4 * 10**9,
        moved=10 * 2**20,
    )(cores, own, other, *rims, own_taps, own_omega)
    gathered = lax.all_to_all(state, PLANE, 0, 0, tiled=True)
    key_map, values = in_main(key_map, values)
    query_map, scores = call(
        scores_kernel,
        [own_spec(0), other_spec(0), rim_spec(0), rim_spec(0), taps_spec(0), OMEGA_SPEC]
        + [head_spec(CHUNK, M)],
        [head_spec(CHUNK, M), head_spec(CHUNK, CHUNK)],
        [main(HEADS, CHUNK, M), main(HEADS, CHUNK, CHUNK)],
        [pltpu.VMEM((RIM + CHUNK, WIDE), f32)],
        flops=8 * 10**9,
        moved=20 * 2**20,
    )(cores, projected, other_q, rims[0], rims[1], conv_filter, frequencies, key_map)
    gathered, query_map, scores = lax.optimization_barrier((gathered, query_map, scores))
    total = small_call(
        total_kernel, [WHOLE], WHOLE, chip(STATE_ROWS, M // 2), [], flops=10**6, moved=2**20
    )(*in_chip(gathered))
    planes = SIZES[0]
    before = [
        lax.ppermute(total, "zh", [(i, i + by) for i in range(planes - by)])
        for by in range(1, planes)
    ]
    prior = small_call(
        prefix_kernel, [WHOLE] * 4, WHOLE, chip(PIECES, STATE_ROWS, M // 2), [],
        flops=10**6, moved=2 * 2**20,
    )(*in_chip(*before, gathered))
    prior = lax.all_to_all(prior, PLANE, 0, 0, tiled=True)
    operands = in_chip(scores, query_map, values, prior)
    attended = small_call(
        attend_other_kernel, [SCALAR] + [WHOLE] * 4, WHOLE, chip(ROWS, COLS), [],
        flops=2 * 10**9, moved=4 * 2**20,
    )(cores, *operands)
    arrived = swap(attended)
    partial = small_call(
        attend_own_kernel, [SCALAR] + [WHOLE] * 4, ANYWHERE, main(ROWS, D),
        [pltpu.VMEM((ROWS, COLS), bf16), pltpu.SemaphoreType.DMA],
        flops=2 * 10**9, moved=4 * 2**20,
    )(cores, *operands)
    return small_call(
        finish_kernel, [SCALAR, WHOLE, ANYWHERE], ANYWHERE, main(ROWS, D),
        [pltpu.SemaphoreType.DMA], flops=0, moved=2**20, aliases={2: 0},
    )(cores, *in_chip(arrived), *in_main(partial))


def solution(mesh):
    devices = Mesh(mesh.devices.reshape(SIZES), AXES)
    placed = (P(None, AXES, None), P(), P())
    return jax.shard_map(
        per_device, mesh=devices, in_specs=placed, out_specs=P(AXES, None), check_vma=False
    )
```

```python
import functools

import jax
import jax.numpy as jnp
from jax import lax
from jax.experimental import pallas as pl
from jax.experimental.pallas import tpu as pltpu
from jax.sharding import Mesh
from jax.sharding import PartitionSpec as P

H = 32
DH = 128
M = 256
KC = 4
D = H * DH

CORES = 2
HEADS = H // CORES
COLS = HEADS * DH
ROWS = 128
CHUNK = CORES * ROWS
RIM = 8
PIECES = 2 * HEADS
STATE_ROWS = DH + 8
GROUP = 4
WIDE = GROUP * DH
STEPS = HEADS // GROUP
FEATURE_SCALE = DH ** (-0.25)
NORM_SCALE = 0.5 * FEATURE_SCALE * FEATURE_SCALE
LOG2_E = 1.4426950408889634
EDGE = 16

AXES = ("zh", "zl", "x", "y", "c")
SIZES = (4, 2, 4, 4, 2)
PLANE = ("zl", "x", "y")

f32 = jnp.float32
bf16 = jnp.bfloat16
NT = (((1,), (1,)), ((), ()))


def dot(a, b):
    return jnp.dot(a, b, preferred_element_type=f32)


def dot_nt(a, b):
    return lax.dot_general(a, b, NT, preferred_element_type=f32)


def fill(core, own, other, rows):
    rows[pl.ds(pl.multiple_of(RIM + core * ROWS, 8), ROWS), :] = own[...].astype(f32)
    rows[pl.ds(pl.multiple_of(RIM + (1 - core) * ROWS, 8), ROWS), :] = other[...].astype(f32)


def convolve(rows, taps, length):
    summed = taps[0:1, :] * rows[RIM : RIM + length, :]
    for j in range(1, KC):
        summed = summed + taps[j : j + 1, :] * rows[RIM - j : RIM - j + length, :]
    return summed.astype(bf16)


def key_features(projection, norm):
    return jnp.exp2(
        projection * (FEATURE_SCALE * LOG2_E) - norm * (NORM_SCALE * LOG2_E)
    ).astype(bf16)


def query_features(projection):
    return jnp.exp2(projection * (FEATURE_SCALE * LOG2_E)).astype(bf16)


def maps_kernel(core_ref, own, other, taps, omega, maps, convolved, rows_k, rows_v):
    core = core_ref[0]
    ones = jnp.ones((M, M), bf16)
    for part in range(GROUP):
        rows_k[part, 0:RIM, :] = jnp.zeros((RIM, DH), f32)
        rows_v[part, 0:RIM, :] = jnp.zeros((RIM, DH), f32)

    def one(group, carried):
        for part in range(GROUP):
            head = group * GROUP + part
            cols = columns(head * DH, DH)
            fill(core, own.at[0, :, cols], other.at[1, :, cols], rows_k.at[part])
            fill(core, own.at[1, :, cols], other.at[2, :, cols], rows_v.at[part])
            k = convolve(rows_k.at[part], taps[1, :, cols], CHUNK)
            convolved[head] = convolve(rows_v.at[part], taps[2, :, cols], CHUNK)
            k_wide = k.astype(f32)
            square = k_wide * k_wide
            upper = square.astype(bf16)
            lower = (square - upper.astype(f32)).astype(bf16)
            norm = dot(jnp.concatenate([upper, lower], axis=1), ones)
            maps[head] = key_features(dot(k, omega[head]), norm)
        return carried

    lax.fori_loop(0, STEPS, one, 0)


def state_kernel(
    core_ref, own, other, rim, taps, omega, maps, convolved,
    state, key_map, values, other_q, rows_k, rows_v, edge_k, edge_v, sems,
):
    core = core_ref[0]
    late = pl.ds(EDGE, CHUNK - EDGE)
    early = pl.ds(0, EDGE)
    moves = [
        pltpu.make_async_copy(maps.at[:, late, :], key_map.at[:, late, :], sems.at[0]),
        pltpu.make_async_copy(convolved.at[:, late, :], values.at[:, late, :], sems.at[1]),
        pltpu.make_async_copy(other.at[pl.ds(0, 1)], other_q, sems.at[2]),
    ]
    for move in moves:
        move.start()

    def edge(group, carried):
        for part in range(GROUP):
            head = group * GROUP + part
            cols = columns(head * DH, DH)
            for which, rows in ((0, rows_k), (1, rows_v)):
                rows[part, 0:RIM, :] = rim[which + 1, :, cols].astype(f32)
                mine = own[which, 0:EDGE, cols].astype(f32)
                theirs = other[which + 1, 0:EDGE, cols].astype(f32)
                rows[part, RIM : RIM + EDGE, :] = jnp.where(core == 0, mine, theirs)
            k = convolve(rows_k.at[part], taps[1, :, cols], EDGE)
            k_wide = k.astype(f32)
            norm = jnp.sum(k_wide * k_wide, axis=1, keepdims=True)
            edge_k[head] = key_features(dot(k, omega[head]), norm)
            edge_v[head] = convolve(rows_v.at[part], taps[2, :, cols], EDGE)
        return carried

    def one(group, carried):
        for part in range(GROUP):
            head = group * GROUP + part
            mapped = jnp.concatenate([edge_k[head], maps[head, EDGE:, :]], axis=0)
            v = jnp.concatenate([edge_v[head], convolved[head, EDGE:, :]], axis=0)
            extended = jnp.concatenate([v.T, jnp.ones((16, CHUNK), bf16)], axis=0)
            sums = dot(extended, mapped)[:STATE_ROWS].astype(bf16)
            state[2 * head] = sums[:, : M // 2]
            state[2 * head + 1] = sums[:, M // 2 :]
        return carried

    lax.fori_loop(0, STEPS, edge, 0, unroll=2)
    last = [
        pltpu.make_async_copy(edge_k, key_map.at[:, early, :], sems.at[3]),
        pltpu.make_async_copy(edge_v, values.at[:, early, :], sems.at[4]),
    ]
    for move in last:
        move.start()
    lax.fori_loop(0, STEPS, one, 0, unroll=2)
    for move in moves + last:
        move.wait()


def scores_kernel(
    core_ref, own_q, other_q, rim_q, taps_q, omega, key_map, query_map, scores, rows_q
):
    core = core_ref[0]
    causal = lax.broadcasted_iota(jnp.int32, (CHUNK, CHUNK), 0) >= lax.broadcasted_iota(
        jnp.int32, (CHUNK, CHUNK), 1
    )
    for head in range(GROUP):
        cols = slice(head * DH, (head + 1) * DH)
        rows_q[head, 0:RIM, :] = rim_q[0, :, cols].astype(f32)
        fill(core, own_q.at[0, :, cols], other_q.at[0, :, cols], rows_q.at[head])
        q = convolve(rows_q.at[head], taps_q[0, :, cols], CHUNK)
        mapped = query_features(dot(q, omega[head]))
        query_map[head] = mapped
        scores[head] = jnp.where(causal, dot_nt(mapped, key_map[head]), 0.0).astype(bf16)


def total_kernel(sums, out):
    total = sums[0].astype(f32)
    for i in range(1, PIECES):
        total = total + sums[i].astype(f32)
    out[...] = total.astype(bf16)


def prefix_kernel(before_1, before_2, before_3, sums, out):
    running = before_1[...].astype(f32) + before_2[...].astype(f32) + before_3[...].astype(f32)
    for i in range(PIECES):
        out[i] = running.astype(bf16)
        running = running + sums[i].astype(f32)


def attend_rows(rows, scores, query_map, values, state, put):
    ones = jnp.ones((CHUNK, DH), bf16)

    def one(head, carried):
        prior = jnp.concatenate([state[2 * head], state[2 * head + 1]], axis=1)
        total = jnp.broadcast_to(prior[DH : DH + 1], (DH, M))
        prior = jnp.concatenate([prior[:DH], total], axis=0)
        both = dot(scores[head, rows, :], jnp.concatenate([values[head], ones], axis=1))
        both = both + dot_nt(query_map[head, rows, :], prior)
        put(head, (both[:, :DH] / both[:, DH:]).astype(bf16))
        return carried

    lax.fori_loop(0, HEADS, one, 0, unroll=4)


def columns(start, size):
    return pl.ds(pl.multiple_of(start, DH), size)


def attend_other_kernel(core_ref, scores, query_map, values, state, out):
    start = pl.multiple_of((1 - core_ref[0]) * ROWS, ROWS)

    def put(head, block):
        out[:, columns(head * DH, DH)] = block

    attend_rows(pl.ds(start, ROWS), scores, query_map, values, state, put)


def attend_own_kernel(core_ref, scores, query_map, values, state, out, block_rows, sem):
    core = core_ref[0]
    start = pl.multiple_of(core * ROWS, ROWS)

    def put(head, block):
        block_rows[:, columns(head * DH, DH)] = block

    attend_rows(pl.ds(start, ROWS), scores, query_map, values, state, put)
    copy = pltpu.make_async_copy(block_rows, out.at[:, columns(core * COLS, COLS)], sem)
    copy.start()
    copy.wait()


def finish_kernel(core_ref, arrived, partial, out, sem):
    copy = pltpu.make_async_copy(arrived, out.at[:, columns((1 - core_ref[0]) * COLS, COLS)], sem)
    copy.start()
    copy.wait()


def run_copies(pairs, sems):
    copies = [
        pltpu.make_async_copy(source, target, sems.at[i])
        for i, (source, target) in enumerate(pairs)
    ]
    for copy in copies:
        copy.start()
    for copy in copies:
        copy.wait()


def split_kernel(core_ref, projected, sent, rim_own, sems):
    core = core_ref[0]
    last = pl.ds(ROWS - RIM, RIM)
    pairs = [
        (projected.at[:, :, columns((1 - core) * COLS, COLS)], sent),
        (projected.at[:, last, columns(core * COLS, COLS)], rim_own),
    ]
    run_copies(pairs, sems)


def rim_kernel(core_ref, rim_own, other, out):
    theirs = other[:, ROWS - RIM :, :]
    out[...] = jnp.where(core_ref[0] == 0, theirs.astype(f32), rim_own[...].astype(f32)).astype(bf16)


def fetch_kernel(core_ref, projected, taps, omega, own, own_taps, own_omega, sems):
    cols = columns(core_ref[0] * COLS, COLS)
    pairs = [
        (projected.at[pl.ds(1, 2), :, cols], own),
        (taps.at[:, :, cols], own_taps),
        (omega.at[pl.ds(core_ref[0] * HEADS, HEADS)], own_omega),
    ]
    run_copies(pairs, sems)


def spec(shape, index):
    return pl.BlockSpec(shape, index)


def own_spec(which):
    return spec((1, ROWS, WIDE), lambda i, core: (which, 0, core[0] * STEPS + i))


def other_spec(which):
    return spec((1, ROWS, WIDE), lambda i, core: (which, 0, i))


def rim_spec(which):
    return spec((1, RIM, WIDE), lambda i, core: (which, 0, i))


def taps_spec(which):
    return spec((1, KC, WIDE), lambda i, core: (which, 0, core[0] * STEPS + i))


OMEGA_SPEC = spec((GROUP, DH, M), lambda i, core: (core[0] * STEPS + i, 0, 0))


def head_spec(*dims):
    return spec((GROUP,) + dims, lambda i, core: (i,) + (0,) * len(dims))


STATE_SPEC = spec((2 * GROUP, STATE_ROWS, M // 2), lambda i, core: (i, 0, 0))
SCALAR = pl.BlockSpec(memory_space=pltpu.SMEM)
WHOLE = pl.BlockSpec(memory_space=pltpu.VMEM)
ANYWHERE = pl.BlockSpec(memory_space=pl.ANY)


def chip(*dims):
    return pltpu.VMEM(dims, bf16)


def main(*dims):
    return pltpu.HBM(dims, bf16)


def in_chip(*arrays):
    return [pltpu.with_memory_space_constraint(a, pltpu.VMEM) for a in arrays]


def in_main(*arrays):
    return [pltpu.with_memory_space_constraint(a, pltpu.HBM) for a in arrays]


def small_call(kernel, in_specs, out_specs, out_shape, scratch, flops, moved, aliases=None):
    return pl.pallas_call(
        kernel,
        in_specs=in_specs,
        out_specs=out_specs,
        out_shape=out_shape,
        scratch_shapes=scratch,
        input_output_aliases=aliases or {},
        compiler_params=pltpu.CompilerParams(vmem_limit_bytes=16 * 2**20),
        cost_estimate=pl.CostEstimate(flops=flops, bytes_accessed=moved, transcendentals=0),
    )


def call(kernel, in_specs, out_specs, out_shape, scratch, flops, moved):
    return pl.pallas_call(
        kernel,
        grid_spec=pltpu.PrefetchScalarGridSpec(
            num_scalar_prefetch=1,
            grid=(STEPS,),
            in_specs=in_specs,
            out_specs=out_specs,
            scratch_shapes=scratch,
        ),
        out_shape=out_shape,
        compiler_params=pltpu.CompilerParams(
            dimension_semantics=("arbitrary",), vmem_limit_bytes=20 * 2**20
        ),
        cost_estimate=pl.CostEstimate(flops=flops, bytes_accessed=moved, transcendentals=0),
    )


def swap(array):
    return lax.ppermute(array, "c", [(0, 1), (1, 0)])


def per_device(projected, conv_filter, frequencies):
    core = lax.axis_index("c").astype(jnp.int32)
    cores = core.reshape(1)
    projected, conv_filter, frequencies = in_main(projected, conv_filter, frequencies)
    sent, rim_own = small_call(
        split_kernel,
        [SCALAR, ANYWHERE],
        [WHOLE] * 2,
        [chip(3, ROWS, COLS), chip(3, RIM, COLS)],
        [pltpu.SemaphoreType.DMA((2,))],
        flops=0,
        moved=3 * 2**20,
    )(cores, projected)
    other = swap(sent)
    (other,) = in_chip(other)
    rim = small_call(
        rim_kernel, [SCALAR, WHOLE, WHOLE], WHOLE, chip(3, RIM, COLS), [], flops=0, moved=2**18
    )(cores, *in_chip(rim_own), other)
    count = 256 - CORES
    rim = lax.ppermute(rim, AXES, [(i, i + CORES) for i in range(count)])
    fetched = small_call(
        fetch_kernel,
        [SCALAR] + [ANYWHERE] * 3,
        [WHOLE] * 3,
        [chip(2, ROWS, COLS), pltpu.VMEM((3, KC, COLS), f32), chip(HEADS, DH, M)],
        [pltpu.SemaphoreType.DMA((3,))],
        flops=0,
        moved=5 * 2**20,
    )(cores, projected, conv_filter, frequencies)
    own, own_taps, own_omega, rim = in_chip(*fetched, rim)
    raw = [pltpu.VMEM((GROUP, RIM + CHUNK, DH), f32)] * 2
    maps, convolved = small_call(
        maps_kernel,
        [SCALAR] + [WHOLE] * 4,
        [WHOLE, WHOLE],
        [chip(HEADS, CHUNK, M), chip(HEADS, CHUNK, DH)],
        raw,
        flops=3 * 10**9,
        moved=6 * 2**20,
    )(cores, own, other, own_taps, own_omega)
    state, key_map, values, other_q = small_call(
        state_kernel,
        [SCALAR] + [WHOLE] * 7,
        [WHOLE] + [ANYWHERE] * 3,
        [chip(PIECES, STATE_ROWS, M // 2), main(HEADS, CHUNK, M), main(HEADS, CHUNK, DH)]
        + [main(1, ROWS, COLS)],
        [pltpu.VMEM((GROUP, RIM + EDGE, DH), f32)] * 2
        + [pltpu.VMEM((HEADS, EDGE, M), bf16), pltpu.VMEM((HEADS, EDGE, DH), bf16)]
        + [pltpu.SemaphoreType.DMA((5,))],
        flops=2 * 10**9,
        moved=6 * 2**20,
    )(cores, own, other, rim, own_taps, own_omega, *in_chip(maps, convolved))
    gathered = lax.all_to_all(state, PLANE, 0, 0, tiled=True)
    key_map, values, other_q = in_main(key_map, values, other_q)
    query_map, scores = call(
        scores_kernel,
        [own_spec(0), other_spec(0), rim_spec(0), taps_spec(0), OMEGA_SPEC]
        + [head_spec(CHUNK, M)],
        [head_spec(CHUNK, M), head_spec(CHUNK, CHUNK)],
        [main(HEADS, CHUNK, M), main(HEADS, CHUNK, CHUNK)],
        [pltpu.VMEM((GROUP, RIM + CHUNK, DH), f32)],
        flops=8 * 10**9,
        moved=20 * 2**20,
    )(cores, projected, other_q, rim, conv_filter, frequencies, key_map)
    gathered, query_map, scores = lax.optimization_barrier((gathered, query_map, scores))
    total = small_call(
        total_kernel, [WHOLE], WHOLE, chip(STATE_ROWS, M // 2), [], flops=10**6, moved=2**20
    )(*in_chip(gathered))
    planes = SIZES[0]
    before = [
        lax.ppermute(total, "zh", [(i, i + by) for i in range(planes - by)])
        for by in range(1, planes)
    ]
    prior = small_call(
        prefix_kernel, [WHOLE] * 4, WHOLE, chip(PIECES, STATE_ROWS, M // 2), [],
        flops=10**6, moved=2 * 2**20,
    )(*in_chip(*before, gathered))
    prior = lax.all_to_all(prior, PLANE, 0, 0, tiled=True)
    operands = in_chip(scores, query_map, values, prior)
    attended = small_call(
        attend_other_kernel, [SCALAR] + [WHOLE] * 4, WHOLE, chip(ROWS, COLS), [],
        flops=2 * 10**9, moved=4 * 2**20,
    )(cores, *operands)
    arrived = swap(attended)
    partial = small_call(
        attend_own_kernel, [SCALAR] + [WHOLE] * 4, ANYWHERE, main(ROWS, D),
        [pltpu.VMEM((ROWS, COLS), bf16), pltpu.SemaphoreType.DMA],
        flops=2 * 10**9, moved=4 * 2**20,
    )(cores, *operands)
    return small_call(
        finish_kernel, [SCALAR, WHOLE, ANYWHERE], ANYWHERE, main(ROWS, D),
        [pltpu.SemaphoreType.DMA], flops=0, moved=2**20, aliases={2: 0},
    )(cores, *in_chip(arrived), *in_main(partial))


def solution(mesh):
    devices = Mesh(mesh.devices.reshape(SIZES), AXES)
    placed = (P(None, AXES, None), P(), P())
    return jax.shard_map(
        per_device, mesh=devices, in_specs=placed, out_specs=P(AXES, None), check_vma=False
    )
```

```python
import functools

import jax
import jax.numpy as jnp
from jax import lax
from jax.experimental import pallas as pl
from jax.experimental.pallas import tpu as pltpu
from jax.sharding import Mesh
from jax.sharding import PartitionSpec as P

H = 32
DH = 128
M = 256
KC = 4
D = H * DH

CORES = 2
HEADS = H // CORES
COLS = HEADS * DH
ROWS = 128
CHUNK = CORES * ROWS
RIM = 8
PIECES = 2 * HEADS
STATE_ROWS = DH + 8
GROUP = 4
WIDE = GROUP * DH
STEPS = HEADS // GROUP
FEATURE_SCALE = DH ** (-0.25)
NORM_SCALE = 0.5 * FEATURE_SCALE * FEATURE_SCALE
LOG2_E = 1.4426950408889634
EDGE = 16

AXES = ("zh", "zl", "x", "y", "c")
SIZES = (4, 2, 4, 4, 2)
PLANE = ("zl", "x", "y")

f32 = jnp.float32
bf16 = jnp.bfloat16
NT = (((1,), (1,)), ((), ()))


def dot(a, b):
    return jnp.dot(a, b, preferred_element_type=f32)


def dot_nt(a, b):
    return lax.dot_general(a, b, NT, preferred_element_type=f32)


def fill(core, own, other, rows):
    rows[pl.ds(pl.multiple_of(RIM + core * ROWS, 8), ROWS), :] = own[...].astype(f32)
    rows[pl.ds(pl.multiple_of(RIM + (1 - core) * ROWS, 8), ROWS), :] = other[...].astype(f32)


def convolve(rows, taps, length):
    summed = taps[0:1, :] * rows[RIM : RIM + length, :]
    for j in range(1, KC):
        summed = summed + taps[j : j + 1, :] * rows[RIM - j : RIM - j + length, :]
    return summed.astype(bf16)


def key_features(projection, norm):
    return jnp.exp2(
        projection * (FEATURE_SCALE * LOG2_E) - norm * (NORM_SCALE * LOG2_E)
    ).astype(bf16)


def query_features(projection):
    return jnp.exp2(projection * (FEATURE_SCALE * LOG2_E)).astype(bf16)


def maps_kernel(core_ref, own, other, taps, omega, maps, convolved, rows_k, rows_v):
    core = core_ref[0]
    ones = jnp.ones((M, M), bf16)
    for part in range(GROUP):
        rows_k[part, 0:RIM, :] = jnp.zeros((RIM, DH), f32)
        rows_v[part, 0:RIM, :] = jnp.zeros((RIM, DH), f32)

    def one(group, carried):
        for part in range(GROUP):
            head = group * GROUP + part
            cols = columns(head * DH, DH)
            fill(core, own.at[0, :, cols], other.at[1, :, cols], rows_k.at[part])
            fill(core, own.at[1, :, cols], other.at[2, :, cols], rows_v.at[part])
            k = convolve(rows_k.at[part], taps[1, :, cols], CHUNK)
            convolved[head] = convolve(rows_v.at[part], taps[2, :, cols], CHUNK)
            k_wide = k.astype(f32)
            square = k_wide * k_wide
            upper = square.astype(bf16)
            lower = (square - upper.astype(f32)).astype(bf16)
            norm = dot(jnp.concatenate([upper, lower], axis=1), ones)
            maps[head] = key_features(dot(k, omega[head]), norm)
        return carried

    lax.fori_loop(0, STEPS, one, 0)


def piece_of(head, flip):
    return lax.rem(2 * head + flip * HEADS, PIECES)


def state_kernel(
    core_ref, flip_ref, own, other, rim, taps, omega, maps, convolved,
    state, key_map, values, other_q, rows_k, rows_v, edge_k, edge_v, sems,
):
    core = core_ref[0]
    late = pl.ds(EDGE, CHUNK - EDGE)
    early = pl.ds(0, EDGE)
    moves = [
        pltpu.make_async_copy(maps.at[:, late, :], key_map.at[:, late, :], sems.at[0]),
        pltpu.make_async_copy(convolved.at[:, late, :], values.at[:, late, :], sems.at[1]),
        pltpu.make_async_copy(other.at[pl.ds(0, 1)], other_q, sems.at[2]),
    ]
    for move in moves:
        move.start()

    def edge(group, carried):
        for part in range(GROUP):
            head = group * GROUP + part
            cols = columns(head * DH, DH)
            for which, rows in ((0, rows_k), (1, rows_v)):
                rows[part, 0:RIM, :] = rim[which + 1, :, cols].astype(f32)
                mine = own[which, 0:EDGE, cols].astype(f32)
                theirs = other[which + 1, 0:EDGE, cols].astype(f32)
                rows[part, RIM : RIM + EDGE, :] = jnp.where(core == 0, mine, theirs)
            k = convolve(rows_k.at[part], taps[1, :, cols], EDGE)
            k_wide = k.astype(f32)
            norm = jnp.sum(k_wide * k_wide, axis=1, keepdims=True)
            edge_k[head] = key_features(dot(k, omega[head]), norm)
            edge_v[head] = convolve(rows_v.at[part], taps[2, :, cols], EDGE)
        return carried

    def one(group, carried):
        for part in range(GROUP):
            head = group * GROUP + part
            mapped = jnp.concatenate([edge_k[head], maps[head, EDGE:, :]], axis=0)
            v = jnp.concatenate([edge_v[head], convolved[head, EDGE:, :]], axis=0)
            extended = jnp.concatenate([v.T, jnp.ones((16, CHUNK), bf16)], axis=0)
            sums = dot(extended, mapped)[:STATE_ROWS].astype(bf16)
            piece = piece_of(head, flip_ref[0])
            state[piece] = sums[:, : M // 2]
            state[piece + 1] = sums[:, M // 2 :]
        return carried

    lax.fori_loop(0, STEPS, edge, 0, unroll=2)
    last = [
        pltpu.make_async_copy(edge_k, key_map.at[:, early, :], sems.at[3]),
        pltpu.make_async_copy(edge_v, values.at[:, early, :], sems.at[4]),
    ]
    for move in last:
        move.start()
    lax.fori_loop(0, STEPS, one, 0, unroll=2)
    for move in moves + last:
        move.wait()


def scores_kernel(
    core_ref, own_q, other_q, rim_q, taps_q, omega, key_map, query_map, scores, rows_q
):
    core = core_ref[0]
    causal = lax.broadcasted_iota(jnp.int32, (CHUNK, CHUNK), 0) >= lax.broadcasted_iota(
        jnp.int32, (CHUNK, CHUNK), 1
    )
    for head in range(GROUP):
        cols = slice(head * DH, (head + 1) * DH)
        rows_q[head, 0:RIM, :] = rim_q[0, :, cols].astype(f32)
        fill(core, own_q.at[0, :, cols], other_q.at[0, :, cols], rows_q.at[head])
        q = convolve(rows_q.at[head], taps_q[0, :, cols], CHUNK)
        mapped = query_features(dot(q, omega[head]))
        query_map[head] = mapped
        scores[head] = jnp.where(causal, dot_nt(mapped, key_map[head]), 0.0).astype(bf16)


def total_kernel(sums, out):
    total = sums[0].astype(f32)
    for i in range(1, PIECES):
        total = total + sums[i].astype(f32)
    out[...] = total.astype(bf16)


def prefix_kernel(before_1, before_2, before_3, sums, out):
    running = before_1[...].astype(f32) + before_2[...].astype(f32) + before_3[...].astype(f32)
    for i in range(PIECES):
        out[i] = running.astype(bf16)
        running = running + sums[i].astype(f32)


def attend_rows(rows, flip, scores, query_map, values, state, put, group):
    ones = jnp.ones((CHUNK, DH), bf16)
    for head in range(group * GROUP, (group + 1) * GROUP):
        piece = piece_of(head, flip)
        prior = jnp.concatenate([state[piece], state[piece + 1]], axis=1)
        total = jnp.broadcast_to(prior[DH : DH + 1], (DH, M))
        prior = jnp.concatenate([prior[:DH], total], axis=0)
        both = dot(scores[head, rows, :], jnp.concatenate([values[head], ones], axis=1))
        both = both + dot_nt(query_map[head, rows, :], prior)
        put(head, (both[:, :DH] / both[:, DH:]).astype(bf16))


def columns(start, size):
    return pl.ds(pl.multiple_of(start, DH), size)


def attend_other_kernel(core_ref, flip_ref, scores, query_map, values, state, out):
    start = pl.multiple_of((1 - core_ref[0]) * ROWS, ROWS)

    def put(head, block):
        out[:, columns(head * DH, DH)] = block

    for group in range(STEPS):
        attend_rows(
            pl.ds(start, ROWS), flip_ref[0], scores, query_map, values, state, put, group
        )


def attend_own_kernel(
    core_ref, flip_ref, scores, query_map, values, state, out, block_rows, sems
):
    core = core_ref[0]
    rows = pl.ds(pl.multiple_of(core * ROWS, ROWS), ROWS)

    def put(head, block):
        block_rows[:, columns(head * DH, DH)] = block

    def copy(group):
        return pltpu.make_async_copy(
            block_rows.at[:, pl.ds(group * WIDE, WIDE)],
            out.at[:, columns(core * COLS + group * WIDE, WIDE)],
            sems.at[group],
        )

    for group in range(STEPS):
        attend_rows(rows, flip_ref[0], scores, query_map, values, state, put, group)
        copy(group).start()
    for group in range(STEPS):
        copy(group).wait()


def finish_kernel(core_ref, arrived, partial, out, sems):
    start = (1 - core_ref[0]) * COLS
    pairs = [
        (
            arrived.at[:, pl.ds(group * WIDE, WIDE)],
            out.at[:, columns(start + group * WIDE, WIDE)],
        )
        for group in range(STEPS)
    ]
    run_copies(pairs, sems)


def run_copies(pairs, sems):
    copies = [
        pltpu.make_async_copy(source, target, sems.at[i])
        for i, (source, target) in enumerate(pairs)
    ]
    for copy in copies:
        copy.start()
    for copy in copies:
        copy.wait()


def split_kernel(core_ref, projected, sent, rim_own, sems):
    core = core_ref[0]
    last = pl.ds(ROWS - RIM, RIM)
    pairs = [
        (projected.at[:, :, columns((1 - core) * COLS, COLS)], sent),
        (projected.at[:, last, columns(core * COLS, COLS)], rim_own),
    ]
    run_copies(pairs, sems)


def rim_kernel(core_ref, rim_own, other, out):
    theirs = other[:, ROWS - RIM :, :]
    out[...] = jnp.where(core_ref[0] == 0, theirs.astype(f32), rim_own[...].astype(f32)).astype(bf16)


def fetch_kernel(core_ref, projected, taps, omega, own, own_taps, own_omega, sems):
    cols = columns(core_ref[0] * COLS, COLS)
    pairs = [
        (projected.at[pl.ds(1, 2), :, cols], own),
        (taps.at[:, :, cols], own_taps),
        (omega.at[pl.ds(core_ref[0] * HEADS, HEADS)], own_omega),
    ]
    run_copies(pairs, sems)


def spec(shape, index):
    return pl.BlockSpec(shape, index)


def own_spec(which):
    return spec((1, ROWS, WIDE), lambda i, core: (which, 0, core[0] * STEPS + i))


def other_spec(which):
    return spec((1, ROWS, WIDE), lambda i, core: (which, 0, i))


def rim_spec(which):
    return spec((1, RIM, WIDE), lambda i, core: (which, 0, i))


def taps_spec(which):
    return spec((1, KC, WIDE), lambda i, core: (which, 0, core[0] * STEPS + i))


OMEGA_SPEC = spec((GROUP, DH, M), lambda i, core: (core[0] * STEPS + i, 0, 0))


def head_spec(*dims):
    return spec((GROUP,) + dims, lambda i, core: (i,) + (0,) * len(dims))


STATE_SPEC = spec((2 * GROUP, STATE_ROWS, M // 2), lambda i, core: (i, 0, 0))
SCALAR = pl.BlockSpec(memory_space=pltpu.SMEM)
WHOLE = pl.BlockSpec(memory_space=pltpu.VMEM)
ANYWHERE = pl.BlockSpec(memory_space=pl.ANY)


def chip(*dims):
    return pltpu.VMEM(dims, bf16)


def main(*dims):
    return pltpu.HBM(dims, bf16)


def in_chip(*arrays):
    return [pltpu.with_memory_space_constraint(a, pltpu.VMEM) for a in arrays]


def in_main(*arrays):
    return [pltpu.with_memory_space_constraint(a, pltpu.HBM) for a in arrays]


def small_call(kernel, in_specs, out_specs, out_shape, scratch, flops, moved, aliases=None):
    return pl.pallas_call(
        kernel,
        in_specs=in_specs,
        out_specs=out_specs,
        out_shape=out_shape,
        scratch_shapes=scratch,
        input_output_aliases=aliases or {},
        compiler_params=pltpu.CompilerParams(vmem_limit_bytes=16 * 2**20),
        cost_estimate=pl.CostEstimate(flops=flops, bytes_accessed=moved, transcendentals=0),
    )


def call(kernel, in_specs, out_specs, out_shape, scratch, flops, moved):
    return pl.pallas_call(
        kernel,
        grid_spec=pltpu.PrefetchScalarGridSpec(
            num_scalar_prefetch=1,
            grid=(STEPS,),
            in_specs=in_specs,
            out_specs=out_specs,
            scratch_shapes=scratch,
        ),
        out_shape=out_shape,
        compiler_params=pltpu.CompilerParams(
            dimension_semantics=("arbitrary",), vmem_limit_bytes=20 * 2**20
        ),
        cost_estimate=pl.CostEstimate(flops=flops, bytes_accessed=moved, transcendentals=0),
    )


def swap(array):
    return lax.ppermute(array, "c", [(0, 1), (1, 0)])


def per_device(projected, conv_filter, frequencies):
    core = lax.axis_index("c").astype(jnp.int32)
    cores = core.reshape(1)
    flips = (lax.axis_index("zh") // 2).astype(jnp.int32).reshape(1)
    projected, conv_filter, frequencies = in_main(projected, conv_filter, frequencies)
    sent, rim_own = small_call(
        split_kernel,
        [SCALAR, ANYWHERE],
        [WHOLE] * 2,
        [chip(3, ROWS, COLS), chip(3, RIM, COLS)],
        [pltpu.SemaphoreType.DMA((2,))],
        flops=0,
        moved=3 * 2**20,
    )(cores, projected)
    other = swap(sent)
    (other,) = in_chip(other)
    rim = small_call(
        rim_kernel, [SCALAR, WHOLE, WHOLE], WHOLE, chip(3, RIM, COLS), [], flops=0, moved=2**18
    )(cores, *in_chip(rim_own), other)
    count = 256 - CORES
    rim = lax.ppermute(rim, AXES, [(i, i + CORES) for i in range(count)])
    fetched = small_call(
        fetch_kernel,
        [SCALAR] + [ANYWHERE] * 3,
        [WHOLE] * 3,
        [chip(2, ROWS, COLS), pltpu.VMEM((3, KC, COLS), f32), chip(HEADS, DH, M)],
        [pltpu.SemaphoreType.DMA((3,))],
        flops=0,
        moved=5 * 2**20,
    )(cores, projected, conv_filter, frequencies)
    own, own_taps, own_omega, rim = in_chip(*fetched, rim)
    raw = [pltpu.VMEM((GROUP, RIM + CHUNK, DH), f32)] * 2
    maps, convolved = small_call(
        maps_kernel,
        [SCALAR] + [WHOLE] * 4,
        [WHOLE, WHOLE],
        [chip(HEADS, CHUNK, M), chip(HEADS, CHUNK, DH)],
        raw,
        flops=3 * 10**9,
        moved=6 * 2**20,
    )(cores, own, other, own_taps, own_omega)
    state, key_map, values, other_q = small_call(
        state_kernel,
        [SCALAR] * 2 + [WHOLE] * 7,
        [WHOLE] + [ANYWHERE] * 3,
        [chip(PIECES, STATE_ROWS, M // 2), main(HEADS, CHUNK, M), main(HEADS, CHUNK, DH)]
        + [main(1, ROWS, COLS)],
        [pltpu.VMEM((GROUP, RIM + EDGE, DH), f32)] * 2
        + [pltpu.VMEM((HEADS, EDGE, M), bf16), pltpu.VMEM((HEADS, EDGE, DH), bf16)]
        + [pltpu.SemaphoreType.DMA((5,))],
        flops=2 * 10**9,
        moved=6 * 2**20,
    )(cores, flips, own, other, rim, own_taps, own_omega, *in_chip(maps, convolved))
    gathered = lax.all_to_all(state, PLANE, 0, 0, tiled=True)
    key_map, values, other_q = in_main(key_map, values, other_q)
    query_map, scores = call(
        scores_kernel,
        [own_spec(0), other_spec(0), rim_spec(0), taps_spec(0), OMEGA_SPEC]
        + [head_spec(CHUNK, M)],
        [head_spec(CHUNK, M), head_spec(CHUNK, CHUNK)],
        [main(HEADS, CHUNK, M), main(HEADS, CHUNK, CHUNK)],
        [pltpu.VMEM((GROUP, RIM + CHUNK, DH), f32)],
        flops=8 * 10**9,
        moved=20 * 2**20,
    )(cores, projected, other_q, rim, conv_filter, frequencies, key_map)
    gathered, query_map, scores = lax.optimization_barrier((gathered, query_map, scores))
    total = small_call(
        total_kernel, [WHOLE], WHOLE, chip(STATE_ROWS, M // 2), [], flops=10**6, moved=2**20
    )(*in_chip(gathered))
    groups = SIZES[0]

    def owner(group, plane):
        return 2 * group + (plane + group // 2) % 2

    before = [
        lax.ppermute(
            total,
            ("zh", "zl"),
            [
                (owner(group, plane), owner(group + by, plane))
                for group in range(groups - by)
                for plane in range(2)
            ],
        )
        for by in reversed(range(1, groups))
    ]
    prior = small_call(
        prefix_kernel, [WHOLE] * 4, WHOLE, chip(PIECES, STATE_ROWS, M // 2), [],
        flops=10**6, moved=2 * 2**20,
    )(*in_chip(*before, gathered))
    prior = lax.all_to_all(prior, PLANE, 0, 0, tiled=True)
    operands = in_chip(scores, query_map, values, prior)
    attended = small_call(
        attend_other_kernel, [SCALAR] * 2 + [WHOLE] * 4, WHOLE, chip(ROWS, COLS), [],
        flops=2 * 10**9, moved=4 * 2**20,
    )(cores, flips, *operands)
    arrived = swap(attended)
    partial = small_call(
        attend_own_kernel, [SCALAR] * 2 + [WHOLE] * 4, ANYWHERE, main(ROWS, D),
        [pltpu.VMEM((ROWS, COLS), bf16), pltpu.SemaphoreType.DMA((STEPS,))],
        flops=2 * 10**9, moved=4 * 2**20,
    )(cores, flips, *operands)
    return small_call(
        finish_kernel, [SCALAR, WHOLE, ANYWHERE], ANYWHERE, main(ROWS, D),
        [pltpu.SemaphoreType.DMA((STEPS,))], flops=0, moved=2**20, aliases={2: 0},
    )(cores, *in_chip(arrived), *in_main(partial))


def solution(mesh):
    devices = Mesh(mesh.devices.reshape(SIZES), AXES)
    placed = (P(None, AXES, None), P(), P())
    return jax.shard_map(
        per_device, mesh=devices, in_specs=placed, out_specs=P(AXES, None), check_vma=False
    )
```

```python
import functools

import jax
import jax.numpy as jnp
from jax import lax
from jax.experimental import pallas as pl
from jax.experimental.pallas import tpu as pltpu
from jax.sharding import Mesh
from jax.sharding import PartitionSpec as P

H = 32
DH = 128
M = 256
KC = 4
D = H * DH

CORES = 2
HEADS = H // CORES
COLS = HEADS * DH
ROWS = 128
CHUNK = CORES * ROWS
RIM = 8
PIECES = 2 * HEADS
STATE_ROWS = DH + 8
GROUP = 4
WIDE = GROUP * DH
STEPS = HEADS // GROUP
FEATURE_SCALE = DH ** (-0.25)
NORM_SCALE = 0.5 * FEATURE_SCALE * FEATURE_SCALE
LOG2_E = 1.4426950408889634
EDGE = 16

AXES = ("zh", "zl", "x", "y", "c")
SIZES = (4, 2, 4, 4, 2)
PLANE = ("zl", "x", "y")

f32 = jnp.float32
bf16 = jnp.bfloat16
NT = (((1,), (1,)), ((), ()))
TN = (((0,), (0,)), ((), ()))


def dot(a, b):
    return jnp.dot(a, b, preferred_element_type=f32)


def dot_nt(a, b):
    return lax.dot_general(a, b, NT, preferred_element_type=f32)


def fill(core, own, other, rows):
    rows[pl.ds(pl.multiple_of(RIM + core * ROWS, 8), ROWS), :] = own[...].astype(f32)
    rows[pl.ds(pl.multiple_of(RIM + (1 - core) * ROWS, 8), ROWS), :] = other[...].astype(f32)


def convolve(rows, taps, length):
    summed = taps[0:1, :] * rows[RIM : RIM + length, :]
    for j in range(1, KC):
        summed = summed + taps[j : j + 1, :] * rows[RIM - j : RIM - j + length, :]
    return summed.astype(bf16)


def key_features(projection, norm):
    return jnp.exp2(
        projection * (FEATURE_SCALE * LOG2_E) - norm * (NORM_SCALE * LOG2_E)
    ).astype(bf16)


def query_features(projection):
    return jnp.exp2(projection * (FEATURE_SCALE * LOG2_E)).astype(bf16)


def key_map_of(k, omega, ones):
    k_wide = k.astype(f32)
    square = k_wide * k_wide
    upper = square.astype(bf16)
    lower = (square - upper.astype(f32)).astype(bf16)
    norm = dot(jnp.concatenate([upper, lower], axis=1), ones)
    return key_features(dot(k, omega), norm)


def maps_kernel(
    core_ref, own, other, taps, omega, partial, other_out, rows_k, rows_v, sem
):
    core = core_ref[0]
    move = pltpu.make_async_copy(other, other_out, sem)
    move.start()
    ones = jnp.ones((M, M), bf16)
    for part in range(GROUP):
        rows_k[part, 0:RIM, :] = jnp.zeros((RIM, DH), f32)
        rows_v[part, 0:RIM, :] = jnp.zeros((RIM, DH), f32)

    def one(group, carried):
        for part in range(GROUP):
            head = group * GROUP + part
            cols = columns(head * DH, DH)
            fill(core, own.at[0, :, cols], other.at[1, :, cols], rows_k.at[part])
            fill(core, own.at[1, :, cols], other.at[2, :, cols], rows_v.at[part])
            k = convolve(rows_k.at[part], taps[1, :, cols], CHUNK)
            v = convolve(rows_v.at[part], taps[2, :, cols], CHUNK)
            extended = jnp.concatenate([v.T, jnp.ones((16, CHUNK), bf16)], axis=0)
            mapped = key_map_of(k, omega[head], ones)
            mapped = jnp.concatenate([jnp.zeros((EDGE, M), bf16), mapped[EDGE:]], axis=0)
            partial[head] = dot(extended, mapped)[:STATE_ROWS]
        return carried

    lax.fori_loop(0, STEPS, one, 0, unroll=2)
    move.wait()


def piece_of(head, flip):
    return lax.rem(2 * head + flip * HEADS, PIECES)


def state_kernel(
    core_ref, flip_ref, own, other, rim, taps, omega, partial, state, rows_k, rows_v
):
    core = core_ref[0]

    flip = flip_ref[0]
    heads = range(HEADS)
    keys, features = [], []
    for head in heads:
        cols = slice(head * DH, (head + 1) * DH)
        for which, rows in ((0, rows_k), (1, rows_v)):
            rows[head, 0:RIM, :] = rim[which + 1, :, cols].astype(f32)
            mine = own[which, 0:EDGE, cols].astype(f32)
            theirs = other[which + 1, 0:EDGE, cols].astype(f32)
            rows[head, RIM : RIM + EDGE, :] = jnp.where(core == 0, mine, theirs)
    for head in heads:
        cols = slice(head * DH, (head + 1) * DH)
        k = convolve(rows_k.at[head], taps[1, :, cols], EDGE)
        k_wide = k.astype(f32)
        keys.append((k, jnp.sum(k_wide * k_wide, axis=1, keepdims=True)))
    for head in heads:
        k, norm = keys[head]
        features.append(key_features(dot(k, omega[head]), norm))
    for head in heads:
        cols = slice(head * DH, (head + 1) * DH)
        v = convolve(rows_v.at[head], taps[2, :, cols], EDGE)
        first = features[head]
        products = lax.dot_general(v, first, TN, preferred_element_type=f32)
        total = jnp.sum(first.astype(f32), axis=0, keepdims=True)
        total = jnp.broadcast_to(total, (STATE_ROWS - DH, M))
        sums = (partial[head] + jnp.concatenate([products, total], axis=0)).astype(bf16)
        piece = piece_of(head, flip)
        state[piece] = sums[:, : M // 2]
        state[piece + 1] = sums[:, M // 2 :]


def scores_kernel(
    core_ref, own_q, own_k, own_v, other_q, other_k, other_v, rim_q, rim_k, rim_v,
    taps_q, taps_k, taps_v, omega, query_map, block, rows_q, rows_k, rows_v,
):
    core = core_ref[0]
    ones = jnp.ones((M, M), bf16)
    causal = lax.broadcasted_iota(jnp.int32, (CHUNK, CHUNK), 0) >= lax.broadcasted_iota(
        jnp.int32, (CHUNK, CHUNK), 1
    )
    for head in range(GROUP):
        cols = slice(head * DH, (head + 1) * DH)
        convolved = []
        for own, other, rim, taps, rows in (
            (own_q, other_q, rim_q, taps_q, rows_q),
            (own_k, other_k, rim_k, taps_k, rows_k),
            (own_v, other_v, rim_v, taps_v, rows_v),
        ):
            rows[head, 0:RIM, :] = rim[0, :, cols].astype(f32)
            fill(core, own.at[0, :, cols], other.at[0, :, cols], rows.at[head])
            convolved.append(convolve(rows.at[head], taps[0, :, cols], CHUNK))
        q, k, v = convolved
        queries = query_features(dot(q, omega[head]))
        query_map[head] = queries
        products = dot_nt(queries, key_map_of(k, omega[head], ones))
        scores = jnp.where(causal, products, 0.0).astype(bf16)
        block[head] = dot(scores, jnp.concatenate([v, ones[:, :DH]], axis=1))


def total_kernel(sums, out):
    total = sums[0].astype(f32)
    for i in range(1, PIECES):
        total = total + sums[i].astype(f32)
    out[...] = total.astype(bf16)


def prefix_kernel(before_1, before_2, before_3, sums, out):
    running = before_1[...].astype(f32) + before_2[...].astype(f32) + before_3[...].astype(f32)
    for i in range(PIECES):
        out[i] = running.astype(bf16)
        running = running + sums[i].astype(f32)


def attend_rows(rows, flip, block, query_map, state, put, group):
    for head in range(group * GROUP, (group + 1) * GROUP):
        piece = piece_of(head, flip)
        prior = jnp.concatenate([state[piece], state[piece + 1]], axis=1)
        total = jnp.broadcast_to(prior[DH : DH + 1], (DH, M))
        prior = jnp.concatenate([prior[:DH], total], axis=0)
        both = block[head, rows, :] + dot_nt(query_map[head, rows, :], prior)
        put(head, (both[:, :DH] / both[:, DH:]).astype(bf16))


def columns(start, size):
    return pl.ds(pl.multiple_of(start, DH), size)


def attend_other_kernel(core_ref, flip_ref, block, query_map, state, out):
    start = pl.multiple_of((1 - core_ref[0]) * ROWS, ROWS)

    def put(head, block):
        out[:, columns(head * DH, DH)] = block

    for group in range(STEPS):
        attend_rows(
            pl.ds(start, ROWS), flip_ref[0], block, query_map, state, put, group
        )


def attend_own_kernel(
    core_ref, flip_ref, block, query_map, state, out, block_rows, sems
):
    core = core_ref[0]
    rows = pl.ds(pl.multiple_of(core * ROWS, ROWS), ROWS)

    def put(head, block):
        block_rows[:, columns(head * DH, DH)] = block

    def copy(group):
        return pltpu.make_async_copy(
            block_rows.at[:, pl.ds(group * WIDE, WIDE)],
            out.at[:, columns(core * COLS + group * WIDE, WIDE)],
            sems.at[group],
        )

    for group in range(STEPS):
        attend_rows(rows, flip_ref[0], block, query_map, state, put, group)
        copy(group).start()
    for group in range(STEPS):
        copy(group).wait()


def finish_kernel(core_ref, arrived, partial, out, sems):
    start = (1 - core_ref[0]) * COLS
    pairs = [
        (
            arrived.at[:, pl.ds(group * WIDE, WIDE)],
            out.at[:, columns(start + group * WIDE, WIDE)],
        )
        for group in range(STEPS)
    ]
    run_copies(pairs, sems)


def run_copies(pairs, sems):
    copies = [
        pltpu.make_async_copy(source, target, sems.at[i])
        for i, (source, target) in enumerate(pairs)
    ]
    for copy in copies:
        copy.start()
    for copy in copies:
        copy.wait()


def split_kernel(core_ref, projected, sent, rim_own, sems):
    core = core_ref[0]
    last = pl.ds(ROWS - RIM, RIM)
    pairs = [
        (projected.at[:, :, columns((1 - core) * COLS, COLS)], sent),
        (projected.at[:, last, columns(core * COLS, COLS)], rim_own),
    ]
    run_copies(pairs, sems)


def rim_kernel(core_ref, rim_own, other, out):
    theirs = other[:, ROWS - RIM :, :]
    out[...] = jnp.where(core_ref[0] == 0, theirs.astype(f32), rim_own[...].astype(f32)).astype(bf16)


def fetch_kernel(core_ref, projected, taps, omega, own, own_taps, own_omega, sems):
    cols = columns(core_ref[0] * COLS, COLS)
    pairs = [
        (projected.at[pl.ds(1, 2), :, cols], own),
        (taps.at[:, :, cols], own_taps),
        (omega.at[pl.ds(core_ref[0] * HEADS, HEADS)], own_omega),
    ]
    run_copies(pairs, sems)


def load_kernel(query_map, block, query_map_out, block_out, sems):
    run_copies([(query_map, query_map_out), (block, block_out)], sems)


def spec(shape, index):
    return pl.BlockSpec(shape, index)


def own_spec(which):
    return spec((1, ROWS, WIDE), lambda i, core: (which, 0, core[0] * STEPS + i))


def other_spec(which):
    return spec((1, ROWS, WIDE), lambda i, core: (which, 0, i))


def rim_spec(which):
    return spec((1, RIM, WIDE), lambda i, core: (which, 0, i))


def taps_spec(which):
    return spec((1, KC, WIDE), lambda i, core: (which, 0, core[0] * STEPS + i))


OMEGA_SPEC = spec((GROUP, DH, M), lambda i, core: (core[0] * STEPS + i, 0, 0))


def head_spec(*dims):
    return spec((GROUP,) + dims, lambda i, core: (i,) + (0,) * len(dims))


STATE_SPEC = spec((2 * GROUP, STATE_ROWS, M // 2), lambda i, core: (i, 0, 0))
SCALAR = pl.BlockSpec(memory_space=pltpu.SMEM)
WHOLE = pl.BlockSpec(memory_space=pltpu.VMEM)
ANYWHERE = pl.BlockSpec(memory_space=pl.ANY)


def chip(*dims):
    return pltpu.VMEM(dims, bf16)


def main(*dims):
    return pltpu.HBM(dims, bf16)


def in_chip(*arrays):
    return [pltpu.with_memory_space_constraint(a, pltpu.VMEM) for a in arrays]


def in_main(*arrays):
    return [pltpu.with_memory_space_constraint(a, pltpu.HBM) for a in arrays]


def small_call(kernel, in_specs, out_specs, out_shape, scratch, flops, moved, aliases=None):
    return pl.pallas_call(
        kernel,
        in_specs=in_specs,
        out_specs=out_specs,
        out_shape=out_shape,
        scratch_shapes=scratch,
        input_output_aliases=aliases or {},
        compiler_params=pltpu.CompilerParams(vmem_limit_bytes=16 * 2**20),
        cost_estimate=pl.CostEstimate(flops=flops, bytes_accessed=moved, transcendentals=0),
    )


def call(kernel, in_specs, out_specs, out_shape, scratch, flops, moved):
    return pl.pallas_call(
        kernel,
        grid_spec=pltpu.PrefetchScalarGridSpec(
            num_scalar_prefetch=1,
            grid=(STEPS,),
            in_specs=in_specs,
            out_specs=out_specs,
            scratch_shapes=scratch,
        ),
        out_shape=out_shape,
        compiler_params=pltpu.CompilerParams(
            dimension_semantics=("arbitrary",), vmem_limit_bytes=20 * 2**20
        ),
        cost_estimate=pl.CostEstimate(flops=flops, bytes_accessed=moved, transcendentals=0),
    )


def swap(array):
    return lax.ppermute(array, "c", [(0, 1), (1, 0)])


def per_device(projected, conv_filter, frequencies):
    core = lax.axis_index("c").astype(jnp.int32)
    cores = core.reshape(1)
    flips = (lax.axis_index("zh") // 2).astype(jnp.int32).reshape(1)
    projected, conv_filter, frequencies = in_main(projected, conv_filter, frequencies)
    sent, rim_own = small_call(
        split_kernel,
        [SCALAR, ANYWHERE],
        [WHOLE] * 2,
        [chip(3, ROWS, COLS), chip(3, RIM, COLS)],
        [pltpu.SemaphoreType.DMA((2,))],
        flops=0,
        moved=3 * 2**20,
    )(cores, projected)
    other = swap(sent)
    (other,) = in_chip(other)
    rim = small_call(
        rim_kernel, [SCALAR, WHOLE, WHOLE], WHOLE, chip(3, RIM, COLS), [], flops=0, moved=2**18
    )(cores, *in_chip(rim_own), other)
    count = 256 - CORES
    rim = lax.ppermute(rim, AXES, [(i, i + CORES) for i in range(count)])
    fetched = small_call(
        fetch_kernel,
        [SCALAR] + [ANYWHERE] * 3,
        [WHOLE] * 3,
        [chip(2, ROWS, COLS), pltpu.VMEM((3, KC, COLS), f32), chip(HEADS, DH, M)],
        [pltpu.SemaphoreType.DMA((3,))],
        flops=0,
        moved=5 * 2**20,
    )(cores, projected, conv_filter, frequencies)
    own, own_taps, own_omega, rim = in_chip(*fetched, rim)
    raw = [pltpu.VMEM((GROUP, RIM + CHUNK, DH), f32)]
    partial, other_main = small_call(
        maps_kernel,
        [SCALAR] + [WHOLE] * 4,
        [WHOLE, ANYWHERE],
        [pltpu.VMEM((HEADS, STATE_ROWS, M), f32), main(3, ROWS, COLS)],
        raw * 2 + [pltpu.SemaphoreType.DMA],
        flops=3 * 10**9,
        moved=6 * 2**20,
    )(cores, own, other, own_taps, own_omega)
    state = small_call(
        state_kernel,
        [SCALAR] * 2 + [WHOLE] * 6,
        WHOLE,
        chip(PIECES, STATE_ROWS, M // 2),
        [pltpu.VMEM((HEADS, RIM + EDGE, DH), f32)] * 2,
        flops=2 * 10**9,
        moved=6 * 2**20,
    )(cores, flips, own, other, rim, own_taps, own_omega, *in_chip(partial))
    gathered = lax.all_to_all(state, PLANE, 0, 0, tiled=True)
    (other_main,) = in_main(other_main)
    which = range(3)
    query_map, block = call(
        scores_kernel,
        [own_spec(w) for w in which]
        + [other_spec(w) for w in which]
        + [rim_spec(w) for w in which]
        + [taps_spec(w) for w in which]
        + [OMEGA_SPEC],
        [head_spec(CHUNK, M), head_spec(CHUNK, 2 * DH)],
        [main(HEADS, CHUNK, M), pltpu.HBM((HEADS, CHUNK, 2 * DH), f32)],
        raw * 3,
        flops=8 * 10**9,
        moved=20 * 2**20,
    )(
        cores, *[projected] * 3, *[other_main] * 3, *[rim] * 3, *[conv_filter] * 3, frequencies
    )
    gathered, query_map, block = lax.optimization_barrier((gathered, query_map, block))
    total = small_call(
        total_kernel, [WHOLE], WHOLE, chip(STATE_ROWS, M // 2), [], flops=10**6, moved=2**20
    )(*in_chip(gathered))
    groups = SIZES[0]

    def owner(group, plane):
        return 2 * group + (plane + group // 2) % 2

    before = [
        lax.ppermute(
            total,
            ("zh", "zl"),
            [
                (owner(group, plane), owner(group + by, plane))
                for group in range(groups - by)
                for plane in range(2)
            ],
        )
        for by in reversed(range(1, groups))
    ]
    prior = small_call(
        prefix_kernel, [WHOLE] * 4, WHOLE, chip(PIECES, STATE_ROWS, M // 2), [],
        flops=10**6, moved=2 * 2**20,
    )(*in_chip(*before, gathered))
    query_map, block = small_call(
        load_kernel, [ANYWHERE] * 2, [WHOLE] * 2,
        [chip(HEADS, CHUNK, M), pltpu.VMEM((HEADS, CHUNK, 2 * DH), f32)],
        [pltpu.SemaphoreType.DMA((2,))], flops=0, moved=12 * 2**20,
    )(*in_main(query_map, block))
    prior, query_map, block = lax.optimization_barrier((prior, query_map, block))
    prior = lax.all_to_all(prior, PLANE, 0, 0, tiled=True)
    operands = in_chip(block, query_map, prior)
    attended = small_call(
        attend_other_kernel, [SCALAR] * 2 + [WHOLE] * 3, WHOLE, chip(ROWS, COLS), [],
        flops=2 * 10**9, moved=4 * 2**20,
    )(cores, flips, *operands)
    arrived = swap(attended)
    partial = small_call(
        attend_own_kernel, [SCALAR] * 2 + [WHOLE] * 3, ANYWHERE, main(ROWS, D),
        [pltpu.VMEM((ROWS, COLS), bf16), pltpu.SemaphoreType.DMA((STEPS,))],
        flops=2 * 10**9, moved=4 * 2**20,
    )(cores, flips, *operands)
    return small_call(
        finish_kernel, [SCALAR, WHOLE, ANYWHERE], ANYWHERE, main(ROWS, D),
        [pltpu.SemaphoreType.DMA((STEPS,))], flops=0, moved=2**20, aliases={2: 0},
    )(cores, *in_chip(arrived), *in_main(partial))


def solution(mesh):
    devices = Mesh(mesh.devices.reshape(SIZES), AXES)
    placed = (P(None, AXES, None), P(), P())
    return jax.shard_map(
        per_device, mesh=devices, in_specs=placed, out_specs=P(AXES, None), check_vma=False
    )
```

```python
import functools

import jax
import jax.numpy as jnp
from jax import lax
from jax.experimental import pallas as pl
from jax.experimental.pallas import tpu as pltpu
from jax.sharding import Mesh
from jax.sharding import PartitionSpec as P

H = 32
DH = 128
M = 256
KC = 4
D = H * DH

CORES = 2
HEADS = H // CORES
COLS = HEADS * DH
ROWS = 128
CHUNK = CORES * ROWS
RIM = 8
PIECES = 2 * HEADS
STATE_ROWS = DH + 8
GROUP = 4
WIDE = GROUP * DH
STEPS = HEADS // GROUP
FEATURE_SCALE = DH ** (-0.25)
NORM_SCALE = 0.5 * FEATURE_SCALE * FEATURE_SCALE
LOG2_E = 1.4426950408889634
EDGE = 16

AXES = ("zh", "zl", "x", "y", "c")
SIZES = (4, 2, 4, 4, 2)
PLANE = ("zl", "x", "y")

f32 = jnp.float32
bf16 = jnp.bfloat16
NT = (((1,), (1,)), ((), ()))
TN = (((0,), (0,)), ((), ()))


def dot(a, b):
    return jnp.dot(a, b, preferred_element_type=f32)


def dot_nt(a, b):
    return lax.dot_general(a, b, NT, preferred_element_type=f32)


def fill(core, own, other, rows):
    rows[pl.ds(pl.multiple_of(RIM + core * ROWS, 8), ROWS), :] = own[...].astype(f32)
    rows[pl.ds(pl.multiple_of(RIM + (1 - core) * ROWS, 8), ROWS), :] = other[...].astype(f32)


def convolve(rows, taps, length):
    summed = taps[0:1, :] * rows[RIM : RIM + length, :]
    for j in range(1, KC):
        summed = summed + taps[j : j + 1, :] * rows[RIM - j : RIM - j + length, :]
    return summed.astype(bf16)


def key_features(projection, norm):
    return jnp.exp2(
        projection * (FEATURE_SCALE * LOG2_E) - norm * (NORM_SCALE * LOG2_E)
    ).astype(bf16)


def query_features(projection):
    return jnp.exp2(projection * (FEATURE_SCALE * LOG2_E)).astype(bf16)


def key_map_of(k, omega, ones):
    k_wide = k.astype(f32)
    square = k_wide * k_wide
    upper = square.astype(bf16)
    lower = (square - upper.astype(f32)).astype(bf16)
    norm = dot(jnp.concatenate([upper, lower], axis=1), ones)
    return key_features(dot(k, omega), norm)


def maps_kernel(
    core_ref, own, other, taps, omega, partial, other_out, rows_k, rows_v, sem
):
    core = core_ref[0]
    move = pltpu.make_async_copy(other, other_out, sem)
    move.start()
    ones = jnp.ones((M, M), bf16)
    for part in range(GROUP):
        rows_k[part, 0:RIM, :] = jnp.zeros((RIM, DH), f32)
        rows_v[part, 0:RIM, :] = jnp.zeros((RIM, DH), f32)

    def one(group, carried):
        for part in range(GROUP):
            head = group * GROUP + part
            cols = columns(head * DH, DH)
            fill(core, own.at[0, :, cols], other.at[1, :, cols], rows_k.at[part])
            fill(core, own.at[1, :, cols], other.at[2, :, cols], rows_v.at[part])
            k = convolve(rows_k.at[part], taps[1, :, cols], CHUNK)
            v = convolve(rows_v.at[part], taps[2, :, cols], CHUNK)
            extended = jnp.concatenate([v.T, jnp.ones((16, CHUNK), bf16)], axis=0)
            mapped = key_map_of(k, omega[head], ones)
            mapped = jnp.concatenate([jnp.zeros((EDGE, M), bf16), mapped[EDGE:]], axis=0)
            partial[head] = dot(extended, mapped)[:STATE_ROWS]
        return carried

    lax.fori_loop(0, STEPS, one, 0, unroll=2)
    move.wait()


def piece_of(head, flip):
    return lax.rem(2 * head + flip * HEADS, PIECES)


def state_kernel(
    core_ref, flip_ref, own, other, rim, taps, omega, partial, state, rows_k, rows_v
):
    core = core_ref[0]

    flip = flip_ref[0]
    heads = range(HEADS)
    keys, features = [], []
    for head in heads:
        cols = slice(head * DH, (head + 1) * DH)
        for which, rows in ((0, rows_k), (1, rows_v)):
            rows[head, 0:RIM, :] = rim[which + 1, :, cols].astype(f32)
            mine = own[which, 0:EDGE, cols].astype(f32)
            theirs = other[which + 1, 0:EDGE, cols].astype(f32)
            rows[head, RIM : RIM + EDGE, :] = jnp.where(core == 0, mine, theirs)
    for head in heads:
        cols = slice(head * DH, (head + 1) * DH)
        k = convolve(rows_k.at[head], taps[1, :, cols], EDGE)
        k_wide = k.astype(f32)
        keys.append((k, jnp.sum(k_wide * k_wide, axis=1, keepdims=True)))
    for head in heads:
        k, norm = keys[head]
        features.append(key_features(dot(k, omega[head]), norm))
    for head in heads:
        cols = slice(head * DH, (head + 1) * DH)
        v = convolve(rows_v.at[head], taps[2, :, cols], EDGE)
        first = features[head]
        products = lax.dot_general(v, first, TN, preferred_element_type=f32)
        total = jnp.sum(first.astype(f32), axis=0, keepdims=True)
        total = jnp.broadcast_to(total, (STATE_ROWS - DH, M))
        sums = (partial[head] + jnp.concatenate([products, total], axis=0)).astype(bf16)
        piece = piece_of(head, flip)
        state[piece] = sums[:, : M // 2]
        state[piece + 1] = sums[:, M // 2 :]


def scores_kernel(
    core_ref, own_q, own_k, own_v, other_q, other_k, other_v, rim_q, rim_k, rim_v,
    taps_q, taps_k, taps_v, omega, query_map, block, rows_q, rows_k, rows_v,
):
    core = core_ref[0]
    ones = jnp.ones((M, M), bf16)
    causal = lax.broadcasted_iota(jnp.int32, (CHUNK, CHUNK), 0) >= lax.broadcasted_iota(
        jnp.int32, (CHUNK, CHUNK), 1
    )
    for head in range(GROUP):
        cols = slice(head * DH, (head + 1) * DH)
        convolved = []
        for own, other, rim, taps, rows in (
            (own_q, other_q, rim_q, taps_q, rows_q),
            (own_k, other_k, rim_k, taps_k, rows_k),
            (own_v, other_v, rim_v, taps_v, rows_v),
        ):
            rows[head, 0:RIM, :] = rim[0, :, cols].astype(f32)
            fill(core, own.at[0, :, cols], other.at[0, :, cols], rows.at[head])
            convolved.append(convolve(rows.at[head], taps[0, :, cols], CHUNK))
        q, k, v = convolved
        queries = query_features(dot(q, omega[head]))
        query_map[head] = queries
        products = dot_nt(queries, key_map_of(k, omega[head], ones))
        scores = jnp.where(causal, products, 0.0).astype(bf16)
        block[head] = dot(scores, jnp.concatenate([v, ones[:, :DH]], axis=1))


def total_kernel(sums, out):
    total = sums[0].astype(f32)
    for i in range(1, PIECES):
        total = total + sums[i].astype(f32)
    out[...] = total.astype(bf16)


def pair_kernel(own, before, out):
    out[...] = (own[...].astype(f32) + before[...].astype(f32)).astype(bf16)


def prefix_kernel(before_1, before_2, before_3, sums, out):
    running = before_1[...].astype(f32) + before_2[...].astype(f32) + before_3[...].astype(f32)
    for i in range(PIECES):
        out[i] = running.astype(bf16)
        running = running + sums[i].astype(f32)


def attend_rows(rows, flip, block, query_map, state, put, group):
    for head in range(group * GROUP, (group + 1) * GROUP):
        piece = piece_of(head, flip)
        prior = jnp.concatenate([state[piece], state[piece + 1]], axis=1)
        total = jnp.broadcast_to(prior[DH : DH + 1], (DH, M))
        prior = jnp.concatenate([prior[:DH], total], axis=0)
        both = block[head, rows, :] + dot_nt(query_map[head, rows, :], prior)
        put(head, (both[:, :DH] / both[:, DH:]).astype(bf16))


def columns(start, size):
    return pl.ds(pl.multiple_of(start, DH), size)


def attend_other_kernel(core_ref, flip_ref, block, query_map, state, out):
    start = pl.multiple_of((1 - core_ref[0]) * ROWS, ROWS)

    def put(head, block):
        out[:, columns(head * DH, DH)] = block

    for group in range(STEPS):
        attend_rows(
            pl.ds(start, ROWS), flip_ref[0], block, query_map, state, put, group
        )


def attend_own_kernel(
    core_ref, flip_ref, block, query_map, state, out, block_rows, sems
):
    core = core_ref[0]
    rows = pl.ds(pl.multiple_of(core * ROWS, ROWS), ROWS)

    def put(head, block):
        block_rows[:, columns(head * DH, DH)] = block

    def copy(group):
        return pltpu.make_async_copy(
            block_rows.at[:, pl.ds(group * WIDE, WIDE)],
            out.at[:, columns(core * COLS + group * WIDE, WIDE)],
            sems.at[group],
        )

    for group in range(STEPS):
        attend_rows(rows, flip_ref[0], block, query_map, state, put, group)
        copy(group).start()
    for group in range(STEPS):
        copy(group).wait()


def finish_kernel(core_ref, arrived, partial, out, sems):
    start = (1 - core_ref[0]) * COLS
    pairs = [
        (
            arrived.at[:, pl.ds(group * WIDE, WIDE)],
            out.at[:, columns(start + group * WIDE, WIDE)],
        )
        for group in range(STEPS)
    ]
    run_copies(pairs, sems)


def run_copies(pairs, sems):
    copies = [
        pltpu.make_async_copy(source, target, sems.at[i])
        for i, (source, target) in enumerate(pairs)
    ]
    for copy in copies:
        copy.start()
    for copy in copies:
        copy.wait()


def split_kernel(core_ref, projected, sent, rim_own, sems):
    core = core_ref[0]
    last = pl.ds(ROWS - RIM, RIM)
    pairs = [
        (projected.at[:, :, columns((1 - core) * COLS, COLS)], sent),
        (projected.at[:, last, columns(core * COLS, COLS)], rim_own),
    ]
    run_copies(pairs, sems)


def rim_kernel(core_ref, rim_own, other, out):
    theirs = other[:, ROWS - RIM :, :]
    out[...] = jnp.where(core_ref[0] == 0, theirs.astype(f32), rim_own[...].astype(f32)).astype(bf16)


def fetch_kernel(core_ref, projected, taps, omega, own, own_taps, own_omega, sems):
    cols = columns(core_ref[0] * COLS, COLS)
    pairs = [
        (projected.at[pl.ds(1, 2), :, cols], own),
        (taps.at[:, :, cols], own_taps),
        (omega.at[pl.ds(core_ref[0] * HEADS, HEADS)], own_omega),
    ]
    run_copies(pairs, sems)


def load_kernel(query_map, block, query_map_out, block_out, sems):
    run_copies([(query_map, query_map_out), (block, block_out)], sems)


def spec(shape, index):
    return pl.BlockSpec(shape, index)


def own_spec(which):
    return spec((1, ROWS, WIDE), lambda i, core: (which, 0, core[0] * STEPS + i))


def other_spec(which):
    return spec((1, ROWS, WIDE), lambda i, core: (which, 0, i))


def rim_spec(which):
    return spec((1, RIM, WIDE), lambda i, core: (which, 0, i))


def taps_spec(which):
    return spec((1, KC, WIDE), lambda i, core: (which, 0, core[0] * STEPS + i))


OMEGA_SPEC = spec((GROUP, DH, M), lambda i, core: (core[0] * STEPS + i, 0, 0))


def head_spec(*dims):
    return spec((GROUP,) + dims, lambda i, core: (i,) + (0,) * len(dims))


STATE_SPEC = spec((2 * GROUP, STATE_ROWS, M // 2), lambda i, core: (i, 0, 0))
SCALAR = pl.BlockSpec(memory_space=pltpu.SMEM)
WHOLE = pl.BlockSpec(memory_space=pltpu.VMEM)
ANYWHERE = pl.BlockSpec(memory_space=pl.ANY)


def chip(*dims):
    return pltpu.VMEM(dims, bf16)


def main(*dims):
    return pltpu.HBM(dims, bf16)


def in_chip(*arrays):
    return [pltpu.with_memory_space_constraint(a, pltpu.VMEM) for a in arrays]


def in_main(*arrays):
    return [pltpu.with_memory_space_constraint(a, pltpu.HBM) for a in arrays]


def small_call(kernel, in_specs, out_specs, out_shape, scratch, flops, moved, aliases=None):
    return pl.pallas_call(
        kernel,
        in_specs=in_specs,
        out_specs=out_specs,
        out_shape=out_shape,
        scratch_shapes=scratch,
        input_output_aliases=aliases or {},
        compiler_params=pltpu.CompilerParams(vmem_limit_bytes=16 * 2**20),
        cost_estimate=pl.CostEstimate(flops=flops, bytes_accessed=moved, transcendentals=0),
    )


def call(kernel, in_specs, out_specs, out_shape, scratch, flops, moved):
    return pl.pallas_call(
        kernel,
        grid_spec=pltpu.PrefetchScalarGridSpec(
            num_scalar_prefetch=1,
            grid=(STEPS,),
            in_specs=in_specs,
            out_specs=out_specs,
            scratch_shapes=scratch,
        ),
        out_shape=out_shape,
        compiler_params=pltpu.CompilerParams(
            dimension_semantics=("arbitrary",), vmem_limit_bytes=20 * 2**20
        ),
        cost_estimate=pl.CostEstimate(flops=flops, bytes_accessed=moved, transcendentals=0),
    )


def swap(array):
    return lax.ppermute(array, "c", [(0, 1), (1, 0)])


def per_device(projected, conv_filter, frequencies):
    core = lax.axis_index("c").astype(jnp.int32)
    cores = core.reshape(1)
    flips = (lax.axis_index("zh") // 2).astype(jnp.int32).reshape(1)
    projected, conv_filter, frequencies = in_main(projected, conv_filter, frequencies)
    sent, rim_own = small_call(
        split_kernel,
        [SCALAR, ANYWHERE],
        [WHOLE] * 2,
        [chip(3, ROWS, COLS), chip(3, RIM, COLS)],
        [pltpu.SemaphoreType.DMA((2,))],
        flops=0,
        moved=3 * 2**20,
    )(cores, projected)
    other = swap(sent)
    (other,) = in_chip(other)
    rim = small_call(
        rim_kernel, [SCALAR, WHOLE, WHOLE], WHOLE, chip(3, RIM, COLS), [], flops=0, moved=2**18
    )(cores, *in_chip(rim_own), other)
    count = 256 - CORES
    rim = lax.ppermute(rim, AXES, [(i, i + CORES) for i in range(count)])
    fetched = small_call(
        fetch_kernel,
        [SCALAR] + [ANYWHERE] * 3,
        [WHOLE] * 3,
        [chip(2, ROWS, COLS), pltpu.VMEM((3, KC, COLS), f32), chip(HEADS, DH, M)],
        [pltpu.SemaphoreType.DMA((3,))],
        flops=0,
        moved=5 * 2**20,
    )(cores, projected, conv_filter, frequencies)
    own, own_taps, own_omega, rim = in_chip(*fetched, rim)
    raw = [pltpu.VMEM((GROUP, RIM + CHUNK, DH), f32)]
    partial, other_main = small_call(
        maps_kernel,
        [SCALAR] + [WHOLE] * 4,
        [WHOLE, ANYWHERE],
        [pltpu.VMEM((HEADS, STATE_ROWS, M), f32), main(3, ROWS, COLS)],
        raw * 2 + [pltpu.SemaphoreType.DMA],
        flops=3 * 10**9,
        moved=6 * 2**20,
    )(cores, own, other, own_taps, own_omega)
    state = small_call(
        state_kernel,
        [SCALAR] * 2 + [WHOLE] * 6,
        WHOLE,
        chip(PIECES, STATE_ROWS, M // 2),
        [pltpu.VMEM((HEADS, RIM + EDGE, DH), f32)] * 2,
        flops=2 * 10**9,
        moved=6 * 2**20,
    )(cores, flips, own, other, rim, own_taps, own_omega, *in_chip(partial))
    gathered = lax.all_to_all(state, PLANE, 0, 0, tiled=True)
    (other_main,) = in_main(other_main)
    which = range(3)
    query_map, block = call(
        scores_kernel,
        [own_spec(w) for w in which]
        + [other_spec(w) for w in which]
        + [rim_spec(w) for w in which]
        + [taps_spec(w) for w in which]
        + [OMEGA_SPEC],
        [head_spec(CHUNK, M), head_spec(CHUNK, 2 * DH)],
        [main(HEADS, CHUNK, M), pltpu.HBM((HEADS, CHUNK, 2 * DH), f32)],
        raw * 3,
        flops=8 * 10**9,
        moved=20 * 2**20,
    )(
        cores, *[projected] * 3, *[other_main] * 3, *[rim] * 3, *[conv_filter] * 3, frequencies
    )
    gathered, query_map, block = lax.optimization_barrier((gathered, query_map, block))
    total = small_call(
        total_kernel, [WHOLE], WHOLE, chip(STATE_ROWS, M // 2), [], flops=10**6, moved=2**20
    )(*in_chip(gathered))
    def send(array, *pairs):
        def owner(group, plane):
            return 2 * group + (plane + group // 2) % 2

        ways = [(owner(a, plane), owner(b, plane)) for a, b in pairs for plane in range(2)]
        return lax.ppermute(array, ("zh", "zl"), ways)

    nearest = send(total, (0, 1), (2, 3))
    query_map, block = small_call(
        load_kernel, [ANYWHERE] * 2, [WHOLE] * 2,
        [chip(HEADS, CHUNK, M), pltpu.VMEM((HEADS, CHUNK, 2 * DH), f32)],
        [pltpu.SemaphoreType.DMA((2,))], flops=0, moved=12 * 2**20,
    )(*in_main(query_map, block))
    nearest, query_map, block = lax.optimization_barrier((nearest, query_map, block))
    pair = small_call(
        pair_kernel, [WHOLE] * 2, WHOLE, chip(STATE_ROWS, M // 2), [], flops=10**5, moved=10**5
    )(*in_chip(total, nearest))
    before = [nearest, send(pair, (1, 2)), send(pair, (1, 3))]
    prior = small_call(
        prefix_kernel, [WHOLE] * 4, WHOLE, chip(PIECES, STATE_ROWS, M // 2), [],
        flops=10**6, moved=2 * 2**20,
    )(*in_chip(*before, gathered))
    prior = lax.all_to_all(prior, PLANE, 0, 0, tiled=True)
    operands = in_chip(block, query_map, prior)
    attended = small_call(
        attend_other_kernel, [SCALAR] * 2 + [WHOLE] * 3, WHOLE, chip(ROWS, COLS), [],
        flops=2 * 10**9, moved=4 * 2**20,
    )(cores, flips, *operands)
    arrived = swap(attended)
    partial = small_call(
        attend_own_kernel, [SCALAR] * 2 + [WHOLE] * 3, ANYWHERE, main(ROWS, D),
        [pltpu.VMEM((ROWS, COLS), bf16), pltpu.SemaphoreType.DMA((STEPS,))],
        flops=2 * 10**9, moved=4 * 2**20,
    )(cores, flips, *operands)
    return small_call(
        finish_kernel, [SCALAR, WHOLE, ANYWHERE], ANYWHERE, main(ROWS, D),
        [pltpu.SemaphoreType.DMA((STEPS,))], flops=0, moved=2**20, aliases={2: 0},
    )(cores, *in_chip(arrived), *in_main(partial))


def solution(mesh):
    devices = Mesh(mesh.devices.reshape(SIZES), AXES)
    placed = (P(None, AXES, None), P(), P())
    return jax.shard_map(
        per_device, mesh=devices, in_specs=placed, out_specs=P(AXES, None), check_vma=False
    )
```

```python
import functools

import jax
import jax.numpy as jnp
from jax import lax
from jax.experimental import pallas as pl
from jax.experimental.pallas import tpu as pltpu
from jax.sharding import Mesh
from jax.sharding import PartitionSpec as P

H = 32
DH = 128
M = 256
KC = 4
D = H * DH

CORES = 2
HEADS = H // CORES
COLS = HEADS * DH
ROWS = 128
CHUNK = CORES * ROWS
RIM = 8
PIECES = 2 * HEADS
STATE_ROWS = DH + 8
GROUP = 4
WIDE = GROUP * DH
STEPS = HEADS // GROUP
FEATURE_SCALE = DH ** (-0.25)
NORM_SCALE = 0.5 * FEATURE_SCALE * FEATURE_SCALE
LOG2_E = 1.4426950408889634
EDGE = 16

AXES = ("zh", "zl", "x", "y", "c")
SIZES = (4, 2, 4, 4, 2)
PLANE = ("zl", "x", "y")

f32 = jnp.float32
bf16 = jnp.bfloat16
NT = (((1,), (1,)), ((), ()))
TN = (((0,), (0,)), ((), ()))


def dot(a, b):
    return jnp.dot(a, b, preferred_element_type=f32)


def dot_nt(a, b):
    return lax.dot_general(a, b, NT, preferred_element_type=f32)


def fill(core, own, other, rows):
    rows[pl.ds(pl.multiple_of(RIM + core * ROWS, 8), ROWS), :] = own[...].astype(f32)
    rows[pl.ds(pl.multiple_of(RIM + (1 - core) * ROWS, 8), ROWS), :] = other[...].astype(f32)


def convolve(rows, taps, length):
    summed = taps[0:1, :] * rows[RIM : RIM + length, :]
    for j in range(1, KC):
        summed = summed + taps[j : j + 1, :] * rows[RIM - j : RIM - j + length, :]
    return summed.astype(bf16)


def key_features(projection, norm):
    return jnp.exp2(
        projection * (FEATURE_SCALE * LOG2_E) - norm * (NORM_SCALE * LOG2_E)
    ).astype(bf16)


def query_features(projection):
    return jnp.exp2(projection * (FEATURE_SCALE * LOG2_E)).astype(bf16)


def key_map_of(k, omega, ones):
    k_wide = k.astype(f32)
    square = k_wide * k_wide
    upper = square.astype(bf16)
    lower = (square - upper.astype(f32)).astype(bf16)
    norm = dot(jnp.concatenate([upper, lower], axis=1), ones)
    return key_features(dot(k, omega), norm)


def maps_kernel(
    core_ref, own, other, taps, omega, partial, other_out, rows_k, rows_v, sem
):
    core = core_ref[0]
    move = pltpu.make_async_copy(other, other_out, sem)
    move.start()
    ones = jnp.ones((M, M), bf16)
    for part in range(GROUP):
        rows_k[part, 0:RIM, :] = jnp.zeros((RIM, DH), f32)
        rows_v[part, 0:RIM, :] = jnp.zeros((RIM, DH), f32)

    def one(group, carried):
        for part in range(GROUP):
            head = group * GROUP + part
            cols = columns(head * DH, DH)
            fill(core, own.at[0, :, cols], other.at[1, :, cols], rows_k.at[part])
            fill(core, own.at[1, :, cols], other.at[2, :, cols], rows_v.at[part])
            k = convolve(rows_k.at[part], taps[1, :, cols], CHUNK)
            v = convolve(rows_v.at[part], taps[2, :, cols], CHUNK)
            extended = jnp.concatenate([v.T, jnp.ones((16, CHUNK), bf16)], axis=0)
            mapped = key_map_of(k, omega[head], ones)
            mapped = jnp.concatenate([jnp.zeros((EDGE, M), bf16), mapped[EDGE:]], axis=0)
            partial[head] = dot(extended, mapped)[:STATE_ROWS]
        return carried

    lax.fori_loop(0, STEPS, one, 0, unroll=2)
    move.wait()


def piece_of(head, flip):
    return lax.rem(2 * head + flip * HEADS, PIECES)


def state_kernel(
    core_ref, flip_ref, own, other, rim, taps, omega, partial, state, rows_k, rows_v
):
    core = core_ref[0]

    flip = flip_ref[0]
    heads = range(HEADS)
    keys, features = [], []
    for head in heads:
        cols = slice(head * DH, (head + 1) * DH)
        for which, rows in ((0, rows_k), (1, rows_v)):
            rows[head, 0:RIM, :] = rim[which + 1, :, cols].astype(f32)
            mine = own[which, 0:EDGE, cols].astype(f32)
            theirs = other[which + 1, 0:EDGE, cols].astype(f32)
            rows[head, RIM : RIM + EDGE, :] = jnp.where(core == 0, mine, theirs)
    for head in heads:
        cols = slice(head * DH, (head + 1) * DH)
        k = convolve(rows_k.at[head], taps[1, :, cols], EDGE)
        k_wide = k.astype(f32)
        keys.append((k, jnp.sum(k_wide * k_wide, axis=1, keepdims=True)))
    for head in heads:
        k, norm = keys[head]
        features.append(key_features(dot(k, omega[head]), norm))
    for head in heads:
        cols = slice(head * DH, (head + 1) * DH)
        v = convolve(rows_v.at[head], taps[2, :, cols], EDGE)
        first = features[head]
        products = lax.dot_general(v, first, TN, preferred_element_type=f32)
        total = jnp.sum(first.astype(f32), axis=0, keepdims=True)
        total = jnp.broadcast_to(total, (STATE_ROWS - DH, M))
        sums = (partial[head] + jnp.concatenate([products, total], axis=0)).astype(bf16)
        piece = piece_of(head, flip)
        state[piece] = sums[:, : M // 2]
        state[piece + 1] = sums[:, M // 2 :]


def scores_kernel(
    core_ref, own_q, own_k, own_v, other_q, other_k, other_v, rim_q, rim_k, rim_v,
    taps_q, taps_k, taps_v, omega, query_map, block, sums, rows_q, rows_k, rows_v,
):
    core = core_ref[0]
    ones = jnp.ones((M, M), bf16)
    causal = lax.broadcasted_iota(jnp.int32, (CHUNK, CHUNK), 0) >= lax.broadcasted_iota(
        jnp.int32, (CHUNK, CHUNK), 1
    )
    lane = lax.broadcasted_iota(jnp.int32, (CHUNK, DH), 1)

    @pl.when(pl.program_id(0) == 0)
    def _():
        sums[...] = jnp.zeros_like(sums)

    for head in range(GROUP):
        cols = slice(head * DH, (head + 1) * DH)
        convolved = []
        for own, other, rim, taps, rows in (
            (own_q, other_q, rim_q, taps_q, rows_q),
            (own_k, other_k, rim_k, taps_k, rows_k),
            (own_v, other_v, rim_v, taps_v, rows_v),
        ):
            rows[head, 0:RIM, :] = rim[0, :, cols].astype(f32)
            fill(core, own.at[0, :, cols], other.at[0, :, cols], rows.at[head])
            convolved.append(convolve(rows.at[head], taps[0, :, cols], CHUNK))
        q, k, v = convolved
        queries = query_features(dot(q, omega[head]))
        query_map[head] = queries
        products = dot_nt(queries, key_map_of(k, omega[head], ones))
        scores = jnp.where(causal, products, 0.0).astype(bf16)
        both = dot(scores, jnp.concatenate([v, ones[:, :DH]], axis=1))
        block[head] = both[:, :DH]
        mine = lane == pl.program_id(0) * GROUP + head
        sums[...] = jnp.where(mine, both[:, DH:], sums[...])


def total_kernel(sums, out):
    total = sums[0].astype(f32)
    for i in range(1, PIECES):
        total = total + sums[i].astype(f32)
    out[...] = total.astype(bf16)


def pair_kernel(own, before, out):
    out[...] = (own[...].astype(f32) + before[...].astype(f32)).astype(bf16)


def prefix_kernel(before_1, before_2, before_3, sums, out):
    running = before_1[...].astype(f32) + before_2[...].astype(f32) + before_3[...].astype(f32)
    for i in range(PIECES):
        out[i] = running.astype(bf16)
        running = running + sums[i].astype(f32)


def attend_rows(rows, flip, block, sums, query_map, state, put, group):
    for head in range(group * GROUP, (group + 1) * GROUP):
        piece = piece_of(head, flip)
        prior = jnp.concatenate([state[piece], state[piece + 1]], axis=1)
        total = jnp.broadcast_to(prior[DH : DH + 1], (DH, M))
        prior = jnp.concatenate([prior[:DH], total], axis=0)
        both = dot_nt(query_map[head, rows, :], prior)
        numerator = block[head, rows, :] + both[:, :DH]
        denominator = sums[rows, head : head + 1] + both[:, DH:]
        put(head, (numerator / denominator).astype(bf16))


def columns(start, size):
    return pl.ds(pl.multiple_of(start, DH), size)


def attend_other_kernel(core_ref, flip_ref, block, sums, query_map, state, out):
    start = pl.multiple_of((1 - core_ref[0]) * ROWS, ROWS)

    def put(head, block):
        out[:, columns(head * DH, DH)] = block

    for group in range(STEPS):
        attend_rows(
            pl.ds(start, ROWS), flip_ref[0], block, sums, query_map, state, put, group
        )


def attend_own_kernel(
    core_ref, flip_ref, block, sums, query_map, state, out, block_rows, sems
):
    core = core_ref[0]
    rows = pl.ds(pl.multiple_of(core * ROWS, ROWS), ROWS)

    def put(head, block):
        block_rows[:, columns(head * DH, DH)] = block

    def copy(group):
        return pltpu.make_async_copy(
            block_rows.at[:, pl.ds(group * WIDE, WIDE)],
            out.at[:, columns(core * COLS + group * WIDE, WIDE)],
            sems.at[group],
        )

    for group in range(STEPS):
        attend_rows(rows, flip_ref[0], block, sums, query_map, state, put, group)
        copy(group).start()
    for group in range(STEPS):
        copy(group).wait()


def finish_kernel(core_ref, arrived, partial, out, sems):
    start = (1 - core_ref[0]) * COLS
    pairs = [
        (
            arrived.at[:, pl.ds(group * WIDE, WIDE)],
            out.at[:, columns(start + group * WIDE, WIDE)],
        )
        for group in range(STEPS)
    ]
    run_copies(pairs, sems)


def run_copies(pairs, sems):
    copies = [
        pltpu.make_async_copy(source, target, sems.at[i])
        for i, (source, target) in enumerate(pairs)
    ]
    for copy in copies:
        copy.start()
    for copy in copies:
        copy.wait()


def split_kernel(core_ref, projected, sent, rim_own, sems):
    core = core_ref[0]
    last = pl.ds(ROWS - RIM, RIM)
    others = columns((1 - core) * COLS, COLS)
    pairs = [(projected.at[:, last, columns(core * COLS, COLS)], rim_own)]
    for which in range(3):
        for start in range(0, ROWS, ROWS // 2):
            part = (pl.ds(which, 1), pl.ds(start, ROWS // 2))
            pairs.append((projected.at[(*part, others)], sent.at[part]))
    run_copies(pairs, sems)


def rim_kernel(core_ref, rim_own, other, out):
    theirs = other[:, ROWS - RIM :, :]
    out[...] = jnp.where(core_ref[0] == 0, theirs.astype(f32), rim_own[...].astype(f32)).astype(bf16)


def fetch_kernel(core_ref, projected, taps, omega, own, own_taps, own_omega, sems):
    cols = columns(core_ref[0] * COLS, COLS)
    pairs = [
        (projected.at[pl.ds(1, 2), :, cols], own),
        (taps.at[:, :, cols], own_taps),
        (omega.at[pl.ds(core_ref[0] * HEADS, HEADS)], own_omega),
    ]
    run_copies(pairs, sems)


def spec(shape, index):
    return pl.BlockSpec(shape, index)


def own_spec(which):
    return spec((1, ROWS, WIDE), lambda i, core: (which, 0, core[0] * STEPS + i))


def other_spec(which):
    return spec((1, ROWS, WIDE), lambda i, core: (which, 0, i))


def rim_spec(which):
    return spec((1, RIM, WIDE), lambda i, core: (which, 0, i))


def taps_spec(which):
    return spec((1, KC, WIDE), lambda i, core: (which, 0, core[0] * STEPS + i))


OMEGA_SPEC = spec((GROUP, DH, M), lambda i, core: (core[0] * STEPS + i, 0, 0))


def head_spec(*dims):
    return spec((GROUP,) + dims, lambda i, core: (i,) + (0,) * len(dims))


STATE_SPEC = spec((2 * GROUP, STATE_ROWS, M // 2), lambda i, core: (i, 0, 0))
SCALAR = pl.BlockSpec(memory_space=pltpu.SMEM)
WHOLE = pl.BlockSpec(memory_space=pltpu.VMEM)
ANYWHERE = pl.BlockSpec(memory_space=pl.ANY)


def chip(*dims):
    return pltpu.VMEM(dims, bf16)


def main(*dims):
    return pltpu.HBM(dims, bf16)


def in_chip(*arrays):
    return [pltpu.with_memory_space_constraint(a, pltpu.VMEM) for a in arrays]


def in_main(*arrays):
    return [pltpu.with_memory_space_constraint(a, pltpu.HBM) for a in arrays]


def small_call(kernel, in_specs, out_specs, out_shape, scratch, flops, moved, aliases=None):
    return pl.pallas_call(
        kernel,
        in_specs=in_specs,
        out_specs=out_specs,
        out_shape=out_shape,
        scratch_shapes=scratch,
        input_output_aliases=aliases or {},
        compiler_params=pltpu.CompilerParams(vmem_limit_bytes=16 * 2**20),
        cost_estimate=pl.CostEstimate(flops=flops, bytes_accessed=moved, transcendentals=0),
    )


def call(kernel, in_specs, out_specs, out_shape, scratch, flops, moved):
    return pl.pallas_call(
        kernel,
        grid_spec=pltpu.PrefetchScalarGridSpec(
            num_scalar_prefetch=1,
            grid=(STEPS,),
            in_specs=in_specs,
            out_specs=out_specs,
            scratch_shapes=scratch,
        ),
        out_shape=out_shape,
        compiler_params=pltpu.CompilerParams(
            dimension_semantics=("arbitrary",), vmem_limit_bytes=20 * 2**20
        ),
        cost_estimate=pl.CostEstimate(flops=flops, bytes_accessed=moved, transcendentals=0),
    )


def swap(array):
    return lax.ppermute(array, "c", [(0, 1), (1, 0)])


def per_device(projected, conv_filter, frequencies):
    core = lax.axis_index("c").astype(jnp.int32)
    cores = core.reshape(1)
    flips = (lax.axis_index("zh") // 2).astype(jnp.int32).reshape(1)
    projected, conv_filter, frequencies = in_main(projected, conv_filter, frequencies)
    sent, rim_own = small_call(
        split_kernel,
        [SCALAR, ANYWHERE],
        [WHOLE] * 2,
        [chip(3, ROWS, COLS), chip(3, RIM, COLS)],
        [pltpu.SemaphoreType.DMA((7,))],
        flops=0,
        moved=3 * 2**20,
    )(cores, projected)
    other = swap(sent)
    (other,) = in_chip(other)
    rim = small_call(
        rim_kernel, [SCALAR, WHOLE, WHOLE], WHOLE, chip(3, RIM, COLS), [], flops=0, moved=2**18
    )(cores, *in_chip(rim_own), other)
    count = 256 - CORES
    rim = lax.ppermute(rim, AXES, [(i, i + CORES) for i in range(count)])
    fetched = small_call(
        fetch_kernel,
        [SCALAR] + [ANYWHERE] * 3,
        [WHOLE] * 3,
        [chip(2, ROWS, COLS), pltpu.VMEM((3, KC, COLS), f32), chip(HEADS, DH, M)],
        [pltpu.SemaphoreType.DMA((3,))],
        flops=0,
        moved=5 * 2**20,
    )(cores, projected, conv_filter, frequencies)
    own, own_taps, own_omega, rim = in_chip(*fetched, rim)
    raw = [pltpu.VMEM((GROUP, RIM + CHUNK, DH), f32)]
    partial, other_main = small_call(
        maps_kernel,
        [SCALAR] + [WHOLE] * 4,
        [WHOLE, ANYWHERE],
        [pltpu.VMEM((HEADS, STATE_ROWS, M), f32), main(3, ROWS, COLS)],
        raw * 2 + [pltpu.SemaphoreType.DMA],
        flops=3 * 10**9,
        moved=6 * 2**20,
    )(cores, own, other, own_taps, own_omega)
    state = small_call(
        state_kernel,
        [SCALAR] * 2 + [WHOLE] * 6,
        WHOLE,
        chip(PIECES, STATE_ROWS, M // 2),
        [pltpu.VMEM((HEADS, RIM + EDGE, DH), f32)] * 2,
        flops=2 * 10**9,
        moved=6 * 2**20,
    )(cores, flips, own, other, rim, own_taps, own_omega, *in_chip(partial))
    gathered = lax.all_to_all(state, PLANE, 0, 0, tiled=True)
    (other_main,) = in_main(other_main)
    which = range(3)
    query_map, block, sums = call(
        scores_kernel,
        [own_spec(w) for w in which]
        + [other_spec(w) for w in which]
        + [rim_spec(w) for w in which]
        + [taps_spec(w) for w in which]
        + [OMEGA_SPEC],
        [head_spec(CHUNK, M), head_spec(CHUNK, DH), spec((CHUNK, DH), lambda i, core: (0, 0))],
        [main(HEADS, CHUNK, M), pltpu.HBM((HEADS, CHUNK, DH), f32), pltpu.HBM((CHUNK, DH), f32)],
        raw * 3,
        flops=8 * 10**9,
        moved=20 * 2**20,
    )(
        cores, *[projected] * 3, *[other_main] * 3, *[rim] * 3, *[conv_filter] * 3, frequencies
    )
    gathered, query_map, block, sums = lax.optimization_barrier(
        (gathered, query_map, block, sums)
    )
    total = small_call(
        total_kernel, [WHOLE], WHOLE, chip(STATE_ROWS, M // 2), [], flops=10**6, moved=2**20
    )(*in_chip(gathered))
    def send(array, *pairs):
        def owner(group, plane):
            return 2 * group + (plane + group // 2) % 2

        ways = [(owner(a, plane), owner(b, plane)) for a, b in pairs for plane in range(2)]
        return lax.ppermute(array, ("zh", "zl"), ways)

    nearest = send(total, (0, 1), (1, 2))
    skipping = send(total, (0, 2), (1, 3))
    pair = small_call(
        pair_kernel, [WHOLE] * 2, WHOLE, chip(STATE_ROWS, M // 2), [], flops=10**5, moved=10**5
    )(*in_chip(total, skipping))
    before = [nearest, skipping, send(pair, (2, 3))]
    prior = small_call(
        prefix_kernel, [WHOLE] * 4, WHOLE, chip(PIECES, STATE_ROWS, M // 2), [],
        flops=10**6, moved=2 * 2**20,
    )(*in_chip(*before, gathered))
    prior = lax.all_to_all(prior, PLANE, 0, 0, tiled=True)
    operands = in_chip(block, sums, query_map, prior)
    attended = small_call(
        attend_other_kernel, [SCALAR] * 2 + [WHOLE] * 4, WHOLE, chip(ROWS, COLS), [],
        flops=2 * 10**9, moved=4 * 2**20,
    )(cores, flips, *operands)
    arrived = swap(attended)
    partial = small_call(
        attend_own_kernel, [SCALAR] * 2 + [WHOLE] * 4, ANYWHERE, main(ROWS, D),
        [pltpu.VMEM((ROWS, COLS), bf16), pltpu.SemaphoreType.DMA((STEPS,))],
        flops=2 * 10**9, moved=4 * 2**20,
    )(cores, flips, *operands)
    return small_call(
        finish_kernel, [SCALAR, WHOLE, ANYWHERE], ANYWHERE, main(ROWS, D),
        [pltpu.SemaphoreType.DMA((STEPS,))], flops=0, moved=2**20, aliases={2: 0},
    )(cores, *in_chip(arrived), *in_main(partial))


def solution(mesh):
    devices = Mesh(mesh.devices.reshape(SIZES), AXES)
    placed = (P(None, AXES, None), P(), P())
    return jax.shard_map(
        per_device, mesh=devices, in_specs=placed, out_specs=P(AXES, None), check_vma=False
    )
```

```python
import functools

import jax
import jax.numpy as jnp
from jax import lax
from jax.experimental import pallas as pl
from jax.experimental.pallas import tpu as pltpu
from jax.sharding import Mesh
from jax.sharding import PartitionSpec as P

H = 32
DH = 128
M = 256
KC = 4
D = H * DH

CORES = 2
HEADS = H // CORES
COLS = HEADS * DH
ROWS = 128
CHUNK = CORES * ROWS
RIM = 8
PIECES = 2 * HEADS
STATE_ROWS = DH + 8
GROUP = 4
WIDE = GROUP * DH
STEPS = HEADS // GROUP
FEATURE_SCALE = DH ** (-0.25)
NORM_SCALE = 0.5 * FEATURE_SCALE * FEATURE_SCALE
LOG2_E = 1.4426950408889634
EDGE = 16

AXES = ("zh", "zl", "x", "y", "c")
SIZES = (4, 2, 4, 4, 2)
PLANE = ("zl", "x", "y")

f32 = jnp.float32
bf16 = jnp.bfloat16
NT = (((1,), (1,)), ((), ()))
TN = (((0,), (0,)), ((), ()))


def dot(a, b):
    return jnp.dot(a, b, preferred_element_type=f32)


def dot_nt(a, b):
    return lax.dot_general(a, b, NT, preferred_element_type=f32)


def fill(core, own, other, rows):
    rows[pl.ds(pl.multiple_of(RIM + core * ROWS, 8), ROWS), :] = own[...].astype(f32)
    rows[pl.ds(pl.multiple_of(RIM + (1 - core) * ROWS, 8), ROWS), :] = other[...].astype(f32)


def convolve(rows, taps, length):
    summed = taps[0:1, :] * rows[RIM : RIM + length, :]
    for j in range(1, KC):
        summed = summed + taps[j : j + 1, :] * rows[RIM - j : RIM - j + length, :]
    return summed.astype(bf16)


def key_features(projection, norm):
    return jnp.exp2(
        projection * (FEATURE_SCALE * LOG2_E) - norm * (NORM_SCALE * LOG2_E)
    ).astype(bf16)


def query_features(projection):
    return jnp.exp2(projection * (FEATURE_SCALE * LOG2_E)).astype(bf16)


def key_map_of(k, omega, ones):
    k_wide = k.astype(f32)
    square = k_wide * k_wide
    upper = square.astype(bf16)
    lower = (square - upper.astype(f32)).astype(bf16)
    norm = dot(jnp.concatenate([upper, lower], axis=1), ones)
    return key_features(dot(k, omega), norm)


def maps_kernel(
    core_ref, own, other, taps, omega, partial, other_out, rows_k, rows_v, sem
):
    core = core_ref[0]
    move = pltpu.make_async_copy(other, other_out, sem)
    move.start()
    ones = jnp.ones((M, M), bf16)
    for part in range(GROUP):
        rows_k[part, 0:RIM, :] = jnp.zeros((RIM, DH), f32)
        rows_v[part, 0:RIM, :] = jnp.zeros((RIM, DH), f32)

    def one(group, carried):
        for part in range(GROUP):
            head = group * GROUP + part
            cols = columns(head * DH, DH)
            fill(core, own.at[0, :, cols], other.at[1, :, cols], rows_k.at[part])
            fill(core, own.at[1, :, cols], other.at[2, :, cols], rows_v.at[part])
            k = convolve(rows_k.at[part], taps[1, :, cols], CHUNK)
            v = convolve(rows_v.at[part], taps[2, :, cols], CHUNK)
            extended = jnp.concatenate([v.T, jnp.ones((16, CHUNK), bf16)], axis=0)
            mapped = key_map_of(k, omega[head], ones)
            mapped = jnp.concatenate([jnp.zeros((EDGE, M), bf16), mapped[EDGE:]], axis=0)
            partial[head] = dot(extended, mapped)[:STATE_ROWS]
        return carried

    lax.fori_loop(0, STEPS, one, 0, unroll=2)
    move.wait()


def piece_of(head, flip):
    return lax.rem(2 * head + flip * HEADS, PIECES)


def state_kernel(
    core_ref, flip_ref, own, other, rim, taps, omega, partial, state, rows_k, rows_v
):
    core = core_ref[0]

    flip = flip_ref[0]
    heads = range(HEADS)
    keys, features = [], []
    for head in heads:
        cols = slice(head * DH, (head + 1) * DH)
        for which, rows in ((0, rows_k), (1, rows_v)):
            rows[head, 0:RIM, :] = rim[which + 1, :, cols].astype(f32)
            mine = own[which, 0:EDGE, cols].astype(f32)
            theirs = other[which + 1, 0:EDGE, cols].astype(f32)
            rows[head, RIM : RIM + EDGE, :] = jnp.where(core == 0, mine, theirs)
    for head in heads:
        cols = slice(head * DH, (head + 1) * DH)
        k = convolve(rows_k.at[head], taps[1, :, cols], EDGE)
        k_wide = k.astype(f32)
        keys.append((k, jnp.sum(k_wide * k_wide, axis=1, keepdims=True)))
    for head in heads:
        k, norm = keys[head]
        features.append(key_features(dot(k, omega[head]), norm))
    for head in heads:
        cols = slice(head * DH, (head + 1) * DH)
        v = convolve(rows_v.at[head], taps[2, :, cols], EDGE)
        first = features[head]
        products = lax.dot_general(v, first, TN, preferred_element_type=f32)
        total = jnp.sum(first.astype(f32), axis=0, keepdims=True)
        total = jnp.broadcast_to(total, (STATE_ROWS - DH, M))
        sums = (partial[head] + jnp.concatenate([products, total], axis=0)).astype(bf16)
        piece = piece_of(head, flip)
        state[piece] = sums[:, : M // 2]
        state[piece + 1] = sums[:, M // 2 :]


def scores_kernel(
    core_ref, own_q, own_k, own_v, other_q, other_k, other_v, rim_q, rim_k, rim_v,
    taps_q, taps_k, taps_v, omega, query_map, block, sums, rows_q, rows_k, rows_v,
):
    core = core_ref[0]
    ones = jnp.ones((M, M), bf16)
    causal = lax.broadcasted_iota(jnp.int32, (CHUNK, CHUNK), 0) >= lax.broadcasted_iota(
        jnp.int32, (CHUNK, CHUNK), 1
    )
    lane = lax.broadcasted_iota(jnp.int32, (CHUNK, DH), 1)

    @pl.when(pl.program_id(0) == 0)
    def _():
        sums[...] = jnp.zeros_like(sums)

    for head in range(GROUP):
        cols = slice(head * DH, (head + 1) * DH)
        convolved = []
        for own, other, rim, taps, rows in (
            (own_q, other_q, rim_q, taps_q, rows_q),
            (own_k, other_k, rim_k, taps_k, rows_k),
            (own_v, other_v, rim_v, taps_v, rows_v),
        ):
            rows[head, 0:RIM, :] = rim[0, :, cols].astype(f32)
            fill(core, own.at[0, :, cols], other.at[0, :, cols], rows.at[head])
            convolved.append(convolve(rows.at[head], taps[0, :, cols], CHUNK))
        q, k, v = convolved
        queries = query_features(dot(q, omega[head]))
        query_map[head] = queries
        products = dot_nt(queries, key_map_of(k, omega[head], ones))
        scores = jnp.where(causal, products, 0.0).astype(bf16)
        both = dot(scores, jnp.concatenate([v, ones[:, :DH]], axis=1))
        block[head] = both[:, :DH]
        mine = lane == pl.program_id(0) * GROUP + head
        sums[...] = jnp.where(mine, both[:, DH:], sums[...])


def total_kernel(sums, out):
    total = sums[0].astype(f32)
    for i in range(1, PIECES):
        total = total + sums[i].astype(f32)
    out[...] = total.astype(bf16)


def pair_kernel(own, before, out):
    out[...] = (own[...].astype(f32) + before[...].astype(f32)).astype(bf16)


def prefix_kernel(before_1, before_2, before_3, sums, out):
    running = before_1[...].astype(f32) + before_2[...].astype(f32) + before_3[...].astype(f32)
    for i in range(PIECES):
        out[i] = running.astype(bf16)
        running = running + sums[i].astype(f32)


def attend_rows(rows, flip, block, sums, query_map, state, put, group):
    for head in range(group * GROUP, (group + 1) * GROUP):
        piece = piece_of(head, flip)
        prior = jnp.concatenate([state[piece], state[piece + 1]], axis=1)
        total = jnp.broadcast_to(prior[DH : DH + 1], (DH, M))
        prior = jnp.concatenate([prior[:DH], total], axis=0)
        both = dot_nt(query_map[head, rows, :], prior)
        numerator = block[head, rows, :] + both[:, :DH]
        denominator = sums[rows, head : head + 1] + both[:, DH:]
        put(head, (numerator / denominator).astype(bf16))


def columns(start, size):
    return pl.ds(pl.multiple_of(start, DH), size)


def attend_other_kernel(core_ref, flip_ref, block, sums, query_map, state, out):
    start = pl.multiple_of((1 - core_ref[0]) * ROWS, ROWS)

    def put(head, block):
        out[:, columns(head * DH, DH)] = block

    for group in range(STEPS):
        attend_rows(
            pl.ds(start, ROWS), flip_ref[0], block, sums, query_map, state, put, group
        )


def attend_own_kernel(
    core_ref, flip_ref, block, sums, query_map, state, out, block_rows, sems
):
    core = core_ref[0]
    rows = pl.ds(pl.multiple_of(core * ROWS, ROWS), ROWS)

    def put(head, block):
        block_rows[:, columns(head * DH, DH)] = block

    def copy(group):
        return pltpu.make_async_copy(
            block_rows.at[:, pl.ds(group * WIDE, WIDE)],
            out.at[:, columns(core * COLS + group * WIDE, WIDE)],
            sems.at[group],
        )

    for group in range(STEPS):
        attend_rows(rows, flip_ref[0], block, sums, query_map, state, put, group)
        copy(group).start()
    for group in range(STEPS):
        copy(group).wait()


def finish_kernel(core_ref, arrived, partial, out, sems):
    start = (1 - core_ref[0]) * COLS
    pairs = [
        (
            arrived.at[:, pl.ds(group * WIDE, WIDE)],
            out.at[:, columns(start + group * WIDE, WIDE)],
        )
        for group in range(STEPS)
    ]
    run_copies(pairs, sems)


def run_copies(pairs, sems):
    copies = [
        pltpu.make_async_copy(source, target, sems.at[i])
        for i, (source, target) in enumerate(pairs)
    ]
    for copy in copies:
        copy.start()
    for copy in copies:
        copy.wait()


def split_kernel(core_ref, projected, sent, rim_own, sems):
    core = core_ref[0]
    last = pl.ds(ROWS - RIM, RIM)
    others = columns((1 - core) * COLS, COLS)
    pairs = [(projected.at[:, last, columns(core * COLS, COLS)], rim_own)]
    for which in range(3):
        for start in range(0, ROWS, ROWS // 2):
            part = (pl.ds(which, 1), pl.ds(start, ROWS // 2))
            pairs.append((projected.at[(*part, others)], sent.at[part]))
    run_copies(pairs, sems)


def rim_kernel(core_ref, rim_own, other, out):
    theirs = other[:, ROWS - RIM :, :]
    out[...] = jnp.where(core_ref[0] == 0, theirs.astype(f32), rim_own[...].astype(f32)).astype(bf16)


def fetch_kernel(core_ref, projected, taps, omega, own, own_taps, own_omega, sems):
    cols = columns(core_ref[0] * COLS, COLS)
    pairs = [
        (projected.at[pl.ds(1, 2), :, cols], own),
        (taps.at[:, :, cols], own_taps),
        (omega.at[pl.ds(core_ref[0] * HEADS, HEADS)], own_omega),
    ]
    run_copies(pairs, sems)


def spec(shape, index):
    return pl.BlockSpec(shape, index)


def own_spec(which):
    return spec((1, ROWS, WIDE), lambda i, core: (which, 0, core[0] * STEPS + i))


def other_spec(which):
    return spec((1, ROWS, WIDE), lambda i, core: (which, 0, i))


def rim_spec(which):
    return spec((1, RIM, WIDE), lambda i, core: (which, 0, i))


def taps_spec(which):
    return spec((1, KC, WIDE), lambda i, core: (which, 0, core[0] * STEPS + i))


OMEGA_SPEC = spec((GROUP, DH, M), lambda i, core: (core[0] * STEPS + i, 0, 0))


def head_spec(*dims):
    return spec((GROUP,) + dims, lambda i, core: (i,) + (0,) * len(dims))


STATE_SPEC = spec((2 * GROUP, STATE_ROWS, M // 2), lambda i, core: (i, 0, 0))
SCALAR = pl.BlockSpec(memory_space=pltpu.SMEM)
WHOLE = pl.BlockSpec(memory_space=pltpu.VMEM)
ANYWHERE = pl.BlockSpec(memory_space=pl.ANY)


def chip(*dims):
    return pltpu.VMEM(dims, bf16)


def main(*dims):
    return pltpu.HBM(dims, bf16)


def in_chip(*arrays):
    return [pltpu.with_memory_space_constraint(a, pltpu.VMEM) for a in arrays]


def in_main(*arrays):
    return [pltpu.with_memory_space_constraint(a, pltpu.HBM) for a in arrays]


def small_call(kernel, in_specs, out_specs, out_shape, scratch, flops, moved, aliases=None):
    return pl.pallas_call(
        kernel,
        in_specs=in_specs,
        out_specs=out_specs,
        out_shape=out_shape,
        scratch_shapes=scratch,
        input_output_aliases=aliases or {},
        compiler_params=pltpu.CompilerParams(vmem_limit_bytes=16 * 2**20),
        cost_estimate=pl.CostEstimate(flops=flops, bytes_accessed=moved, transcendentals=0),
    )


def call(kernel, in_specs, out_specs, out_shape, scratch, flops, moved):
    return pl.pallas_call(
        kernel,
        grid_spec=pltpu.PrefetchScalarGridSpec(
            num_scalar_prefetch=1,
            grid=(STEPS,),
            in_specs=in_specs,
            out_specs=out_specs,
            scratch_shapes=scratch,
        ),
        out_shape=out_shape,
        compiler_params=pltpu.CompilerParams(
            dimension_semantics=("arbitrary",), vmem_limit_bytes=20 * 2**20
        ),
        cost_estimate=pl.CostEstimate(flops=flops, bytes_accessed=moved, transcendentals=0),
    )


def swap(array):
    return lax.ppermute(array, "c", [(0, 1), (1, 0)])


def per_device(projected, conv_filter, frequencies):
    core = lax.axis_index("c").astype(jnp.int32)
    cores = core.reshape(1)
    flips = (lax.axis_index("zh") // 2).astype(jnp.int32).reshape(1)
    projected, conv_filter, frequencies = in_main(projected, conv_filter, frequencies)
    sent, rim_own = small_call(
        split_kernel,
        [SCALAR, ANYWHERE],
        [WHOLE] * 2,
        [chip(3, ROWS, COLS), chip(3, RIM, COLS)],
        [pltpu.SemaphoreType.DMA((7,))],
        flops=0,
        moved=3 * 2**20,
    )(cores, projected)
    other = swap(sent)
    (other,) = in_chip(other)
    rim = small_call(
        rim_kernel, [SCALAR, WHOLE, WHOLE], WHOLE, chip(3, RIM, COLS), [], flops=0, moved=2**18
    )(cores, *in_chip(rim_own), other)
    count = 256 - CORES
    rim = lax.ppermute(rim, AXES, [(i, i + CORES) for i in range(count)])
    fetched = small_call(
        fetch_kernel,
        [SCALAR] + [ANYWHERE] * 3,
        [WHOLE] * 3,
        [chip(2, ROWS, COLS), pltpu.VMEM((3, KC, COLS), f32), chip(HEADS, DH, M)],
        [pltpu.SemaphoreType.DMA((3,))],
        flops=0,
        moved=5 * 2**20,
    )(cores, projected, conv_filter, frequencies)
    own, own_taps, own_omega, rim = in_chip(*fetched, rim)
    raw = [pltpu.VMEM((GROUP, RIM + CHUNK, DH), f32)]
    partial, other_main = small_call(
        maps_kernel,
        [SCALAR] + [WHOLE] * 4,
        [WHOLE, ANYWHERE],
        [pltpu.VMEM((HEADS, STATE_ROWS, M), f32), main(3, ROWS, COLS)],
        raw * 2 + [pltpu.SemaphoreType.DMA],
        flops=3 * 10**9,
        moved=6 * 2**20,
    )(cores, own, other, own_taps, own_omega)
    state = small_call(
        state_kernel,
        [SCALAR] * 2 + [WHOLE] * 6,
        WHOLE,
        chip(PIECES, STATE_ROWS, M // 2),
        [pltpu.VMEM((HEADS, RIM + EDGE, DH), f32)] * 2,
        flops=2 * 10**9,
        moved=6 * 2**20,
    )(cores, flips, own, other, rim, own_taps, own_omega, *in_chip(partial))
    gathered = lax.all_to_all(state, PLANE, 0, 0, tiled=True)
    (other_main,) = in_main(other_main)
    which = range(3)
    query_map, block, sums = call(
        scores_kernel,
        [own_spec(w) for w in which]
        + [other_spec(w) for w in which]
        + [rim_spec(w) for w in which]
        + [taps_spec(w) for w in which]
        + [OMEGA_SPEC],
        [head_spec(CHUNK, M), head_spec(CHUNK, DH), spec((CHUNK, DH), lambda i, core: (0, 0))],
        [main(HEADS, CHUNK, M), pltpu.HBM((HEADS, CHUNK, DH), f32), pltpu.HBM((CHUNK, DH), f32)],
        raw * 3,
        flops=8 * 10**9,
        moved=20 * 2**20,
    )(
        cores, *[projected] * 3, *[other_main] * 3, *[rim] * 3, *[conv_filter] * 3, frequencies
    )
    gathered, query_map, block, sums = lax.optimization_barrier(
        (gathered, query_map, block, sums)
    )
    total = small_call(
        total_kernel, [WHOLE], WHOLE, chip(STATE_ROWS, M // 2), [], flops=10**6, moved=2**20
    )(*in_chip(gathered))
    def send(array, *pairs):
        def owner(group, plane):
            return 2 * group + (plane + group // 2) % 2

        ways = [(owner(a, plane), owner(b, plane)) for a, b in pairs for plane in range(2)]
        return lax.ppermute(array, ("zh", "zl"), ways)

    skipping = send(total, (0, 2), (1, 3))
    nearest = send(total, (0, 1), (1, 2))
    pair = small_call(
        pair_kernel, [WHOLE] * 2, WHOLE, chip(STATE_ROWS, M // 2), [], flops=10**5, moved=10**5
    )(*in_chip(total, skipping))
    before = [nearest, skipping, send(pair, (2, 3))]
    prior = small_call(
        prefix_kernel, [WHOLE] * 4, WHOLE, chip(PIECES, STATE_ROWS, M // 2), [],
        flops=10**6, moved=2 * 2**20,
    )(*in_chip(*before, gathered))
    prior = lax.all_to_all(prior, PLANE, 0, 0, tiled=True)
    operands = in_chip(block, sums, query_map, prior)
    attended = small_call(
        attend_other_kernel, [SCALAR] * 2 + [WHOLE] * 4, WHOLE, chip(ROWS, COLS), [],
        flops=2 * 10**9, moved=4 * 2**20,
    )(cores, flips, *operands)
    arrived = swap(attended)
    partial = small_call(
        attend_own_kernel, [SCALAR] * 2 + [WHOLE] * 4, ANYWHERE, main(ROWS, D),
        [pltpu.VMEM((ROWS, COLS), bf16), pltpu.SemaphoreType.DMA((STEPS,))],
        flops=2 * 10**9, moved=4 * 2**20,
    )(cores, flips, *operands)
    return small_call(
        finish_kernel, [SCALAR, WHOLE, ANYWHERE], ANYWHERE, main(ROWS, D),
        [pltpu.SemaphoreType.DMA((STEPS,))], flops=0, moved=2**20, aliases={2: 0},
    )(cores, *in_chip(arrived), *in_main(partial))


def solution(mesh):
    devices = Mesh(mesh.devices.reshape(SIZES), AXES)
    placed = (P(None, AXES, None), P(), P())
    return jax.shard_map(
        per_device, mesh=devices, in_specs=placed, out_specs=P(AXES, None), check_vma=False
    )
```
